128 devices in a mesh: date: 2 (over core), space: 64 (over z, y, x).
Axes of the slice: x: 4, y: 4, z: 4, core: 2. Of those that a mesh axis runs over, the one named last changes fastest.
Arguments:
- acquisitions: bfloat16 [16, 8192, 512], P('date', 'space')
- partner: int32 [16, 9], replicated, may hold values from 0 to 15, as said below
- pair_count: int32 [16], replicated, may hold values from 2 to 9, as said below
- band_low: int32 [16, 9], P('date'), may hold values from 0 to 95
- band_high: int32 [16, 9], P('date'), may hold values from 160 to 256
Outputs:
- coherence: bfloat16 [16, 9, 8192, 512], P('date', None, 'space')
The draws below stay inside these ranges and needn't reach their ends.
Inputs may be any that keep to these rules, and one draw needn't show every extreme that they name: For j < pair_count[d], partner[d, j] is the secondary date of pair j of date d; other slots name any date but no pair. A secondary never lies in its reference's block of 8 dates (one index of date), and the pairs of one block name at most 4 distinct dates of any other block; some two blocks reach 4. The pairs of date d are its first pair_count[d] slots.
All inputs are finite; a program needn't handle non-finite values.
Results may differ from the reference program's by a relative error of at most 0.0085.
Values may be sent and summed in bfloat16 or wider, within the bound.
A program may use at most 192 MiB of HBM per device.

```python
import math
import jax
import jax.numpy as jnp
from jax import lax

RANGE = 256
MAXP = 9
DATES_DEV = 8
DATES = 16
ROWS = 8192


def draw_acquisitions(key, part):
    subkeys = jax.random.split(key, 5)
    shape = (DATES, ROWS, 2 * RANGE)
    common = jax.random.truncated_normal(subkeys[0], -6.0, 6.0, (ROWS, 2 * RANGE), jnp.float32)
    noise_part = jax.random.truncated_normal(subkeys[1], -6.0, 6.0, shape, jnp.float32)
    weight = jax.random.uniform(subkeys[2], (DATES, 1, 1), jnp.float32, 0.3, 0.9)
    scale_low = 0.15
    scale_high = 1.5
    row_scale = jnp.exp(jax.random.uniform(subkeys[3], (DATES, ROWS, 1), jnp.float32, math.log(scale_low), math.log(scale_high)))
    col_part = jnp.exp(jax.random.uniform(subkeys[4], (1, 1, RANGE), jnp.float32, math.log(scale_low), math.log(scale_high)))
    col_scale = jnp.concatenate([col_part, col_part], axis=2)
    mixed_part = weight * common[None] + jnp.sqrt(1.0 - weight * weight) * noise_part
    return (row_scale * col_scale * mixed_part).astype(jnp.bfloat16)


def draw_pair_count(key, part):
    subkeys = jax.random.split(key, 5)
    groups = DATES // DATES_DEV
    busy_group = jax.random.randint(subkeys[0], (groups,), 0, 4) == 0
    forced = jax.random.randint(subkeys[1], (), 0, groups)
    group_ids = jnp.arange(groups, dtype=jnp.int32)
    busy_group = busy_group | (group_ids == forced)
    busy_dates = jnp.repeat(busy_group, DATES_DEV)
    busy_count = jax.random.randint(subkeys[2], (DATES,), 7, MAXP + 1)
    quiet_count = jax.random.randint(subkeys[3], (DATES,), 2, 5)
    counts = jnp.where(busy_dates, busy_count, quiet_count)
    date_ids = jnp.arange(DATES, dtype=jnp.int32)
    counts = jnp.where(date_ids // DATES_DEV == forced, MAXP, counts)
    drawn_date = (forced + 1) % groups * DATES_DEV + jax.random.randint(subkeys[4], (), 0, DATES_DEV)
    counts = jnp.where(date_ids == drawn_date, 2, counts)
    return counts.astype(jnp.int32)


def draw_partner(key, part):
    subkeys = jax.random.split(key, 3)
    groups = DATES // DATES_DEV
    capacity = DATES_DEV // 2
    date_ids = jnp.arange(DATES, dtype=jnp.int32)
    home_block = date_ids // DATES_DEV
    local_index = date_ids % DATES_DEV
    slot_ids = jnp.arange(MAXP, dtype=jnp.int32)
    reach = jax.random.randint(subkeys[0], (groups, MAXP), 1, groups // 2 + 1)
    forward_pick = jax.random.randint(subkeys[1], (groups, MAXP), 0, 2) == 1
    offset_table = jax.random.randint(subkeys[2], (groups, groups), 0, DATES_DEV)
    device_step = reach[home_block]
    forward_ok = home_block[:, None] + device_step < groups
    backward_ok = home_block[:, None] - device_step >= 0
    target_block = jnp.where(forward_pick[home_block] & forward_ok | jnp.logical_not(backward_ok), home_block[:, None] + device_step, home_block[:, None] - device_step)
    block_offset = offset_table[home_block[:, None], target_block]
    within_block = (block_offset + (local_index[:, None] + slot_ids[None, :]) % capacity) % DATES_DEV
    live_partner = (target_block * DATES_DEV + within_block).astype(jnp.int32)
    counts = draw_pair_count(key, part)
    dead_partner = jax.random.randint(jax.random.fold_in(key, 7919), (DATES, MAXP), 0, DATES)
    is_live = slot_ids[None, :] < counts[:, None]
    return jnp.where(is_live, live_partner, dead_partner).astype(jnp.int32)


def touch_ends(values, rng, smallest, largest):
    longest = values.shape.index(max(values.shape))
    spots = []
    for shift in (0, 1):
        where = [jax.random.randint(jax.random.fold_in(rng, axis), (), 0, length) for axis, length in enumerate(values.shape)]
        where[longest] = (where[longest] + shift) % values.shape[longest]
        spots.append(tuple(where))
    return values.at[spots[0]].set(smallest).at[spots[1]].set(largest)


def setup_inputs(seed: int = 0) -> dict:
    key_of = jax.random.split(jax.random.key(seed), 6)
    acquisitions = draw_acquisitions(jax.random.fold_in(key_of[5], 71), 0)
    partner = draw_partner(jax.random.fold_in(key_of[5], 71), 0)
    pair_count = draw_pair_count(jax.random.fold_in(key_of[5], 71), 0)
    band_low = touch_ends(jax.random.randint(key_of[3], (DATES, MAXP), 0, RANGE * 3 // 8), jax.random.fold_in(key_of[3], 1), 0, (RANGE * 3 // 8) - 1).astype(jnp.int32)
    band_high = touch_ends(jax.random.randint(key_of[4], (DATES, MAXP), RANGE * 5 // 8, RANGE + 1), jax.random.fold_in(key_of[4], 1), RANGE * 5 // 8, RANGE).astype(jnp.int32)
    return {"acquisitions": acquisitions, "partner": partner, "pair_count": pair_count, "band_low": band_low, "band_high": band_high}


def tables(range_bins):
    bin_ids = jnp.arange(range_bins, dtype=jnp.int32)
    phase_index = bin_ids[:, None] * bin_ids[None, :] % range_bins
    angles = phase_index.astype(jnp.float32) * (2.0 * math.pi / range_bins)
    cosine = jnp.cos(angles)
    sine_part = jnp.sin(angles)
    forward = jnp.concatenate([jnp.concatenate([cosine, -sine_part], 1), jnp.concatenate([sine_part, cosine], 1)], 0)
    inverse = jnp.concatenate([jnp.concatenate([cosine, sine_part], 1), jnp.concatenate([-sine_part, cosine], 1)], 0)
    return (forward.astype(jnp.bfloat16), inverse.astype(jnp.bfloat16))

def window_sums(stacked_field, range_bins):
    widened = jnp.pad(stacked_field, [(0, 0)] * (stacked_field.ndim - 1) + [(4, 4)])
    across = widened[..., 0:range_bins]
    for offset_col in range(1, 9):
        across = across + widened[..., offset_col:offset_col + range_bins]
    return across[..., :-2, :] + across[..., 1:-1, :] + across[..., 2:, :]

def reference(acquisitions, partner, pair_count, band_low, band_high):
    forward, inverse = tables(RANGE)
    range_cols = 2 * RANGE
    spectra = jnp.dot(acquisitions.reshape(-1, range_cols), forward, preferred_element_type=jnp.float32)
    spectra = spectra.astype(jnp.bfloat16).reshape(DATES, ROWS, range_cols)
    bin_index = jnp.arange(range_cols, dtype=jnp.int32) % RANGE
    inverse_size = 1.0 / RANGE

    def one_pair(pair_index):
        date_id = pair_index // MAXP
        slot_id = pair_index % MAXP
        is_live = slot_id < pair_count[date_id]

        def compute_pair():
            second = partner[date_id, slot_id]
            low_bin = band_low[date_id, slot_id]
            high_bin = band_high[date_id, slot_id]
            band_mask = ((bin_index >= low_bin) & (bin_index < high_bin)).astype(jnp.bfloat16)
            ref_spec = lax.dynamic_index_in_dim(spectra, date_id, 0, keepdims=False) * band_mask
            sec_spec = lax.dynamic_index_in_dim(spectra, second, 0, keepdims=False) * band_mask
            filt_ref = jnp.dot(ref_spec, inverse, preferred_element_type=jnp.float32) * inverse_size
            filt_sec = jnp.dot(sec_spec, inverse, preferred_element_type=jnp.float32) * inverse_size
            ref_re, ref_im = (filt_ref[:, :RANGE], filt_ref[:, RANGE:])
            sec_re, sec_im = (filt_sec[:, :RANGE], filt_sec[:, RANGE:])
            fields = jnp.stack([ref_re * sec_re + ref_im * sec_im, ref_im * sec_re - ref_re * sec_im, ref_re * ref_re + ref_im * ref_im, sec_re * sec_re + sec_im * sec_im])
            framed = jnp.pad(fields, ((0, 0), (1, 1), (0, 0)))
            looked = window_sums(framed, RANGE)
            normalizer = 1.0 / jnp.sqrt(jnp.maximum(looked[2], 1.0) * jnp.maximum(looked[3], 1.0))
            return jnp.concatenate([looked[0] * normalizer, looked[1] * normalizer], -1).astype(jnp.bfloat16)

        def empty_out():
            return jnp.zeros((ROWS, range_cols), jnp.bfloat16)
        return lax.cond(is_live, compute_pair, empty_out)
    result = lax.map(one_pair, jnp.arange(DATES * MAXP, dtype=jnp.int32))
    return result.reshape(DATES, MAXP, ROWS, range_cols)
```

```python
import functools
import math

import jax
import jax.numpy as jnp
import numpy as np
from jax import lax
from jax.experimental import pallas as pl
from jax.experimental.pallas import tpu as pltpu
from jax.sharding import PartitionSpec as P

F32 = jnp.float32
BF16 = jnp.bfloat16


def tables(bins):
    ids = np.arange(bins)
    angles = (ids[:, None] * ids[None, :] % bins) * (2.0 * math.pi / bins)
    cosine, sine = np.cos(angles), np.sin(angles)
    forward = np.block([[cosine, -sine], [sine, cosine]])
    inverse = np.block([[cosine, sine], [-sine, cosine]]) / bins
    half = bins // 2
    rows = np.concatenate([np.arange(half), bins + np.arange(half)])
    even = np.concatenate([np.arange(0, bins, 2), bins + np.arange(0, bins, 2)])
    odd = even + 1
    order = np.concatenate([np.arange(0, bins, 2), np.arange(1, bins, 2)])
    window = (np.abs(order[:, None] - ids[None, :]) <= 4).astype(np.float32)
    return (
        jnp.asarray(forward, BF16),
        jnp.asarray(inverse[rows][:, even], BF16),
        jnp.asarray(inverse[rows][:, odd], BF16),
        jnp.asarray(window, BF16),
    )


def exchange_kernel(
    acq_ref, fwd_ref, spec_ref, other, edge_f, edge, halo, halo_f, grid_f, send, recv
):
    dates, rows, cols = acq_ref.shape
    quarters = cols // 128
    date = lax.axis_index("date")
    space = lax.axis_index("space")
    count = lax.axis_size("space")
    before = lax.rem(space + count - 1, count)
    after = lax.rem(space + 1, count)
    far = 1 - date

    barrier = pltpu.get_barrier_semaphore()
    peers = ((far, space), (date, before), (date, after), (far, before), (far, after))
    for peer in peers:
        pl.semaphore_signal(barrier, inc=1, device_id=peer, device_id_type=pl.DeviceIdType.MESH)
    for d in range(dates):
        edge_f[0, d : d + 1, :] = acq_ref[d, 0:16, :].astype(F32)[0:1]
        edge_f[1, d : d + 1, :] = acq_ref[d, rows - 16 : rows, :].astype(F32)[15:16]
    edge[...] = edge_f[...].astype(BF16)
    pl.semaphore_wait(barrier, len(peers))

    def remote(src, dst, k, peer):
        copy = pltpu.make_async_remote_copy(
            src_ref=src,
            dst_ref=dst,
            send_sem=send.at[k],
            recv_sem=recv.at[k],
            device_id=peer,
            device_id_type=pl.DeviceIdType.MESH,
        )
        copy.start()
        return copy

    small = [
        remote(edge.at[1], halo.at[0], 0, (date, after)),
        remote(edge.at[0], halo.at[1], 1, (date, before)),
        remote(edge.at[1], halo.at[2], 2, (far, after)),
        remote(edge.at[0], halo.at[3], 3, (far, before)),
    ]
    big = remote(acq_ref, other, 4, (far, space))

    for copy in small:
        copy.wait()
    top = (space > 0).astype(F32)
    bottom = (space < count - 1).astype(F32)
    for k in range(4):
        block = jnp.dot(halo[k], fwd_ref[...], preferred_element_type=F32)
        halo_f[k] = block * (top if k % 2 == 0 else bottom)

    def place(source, base, halo_base):
        @pl.loop(0, dates)
        def _(i):
            block = jnp.dot(source[i], fwd_ref[...], preferred_element_type=F32)
            first = halo_f[halo_base, pl.ds(i, 1), :]
            last = halo_f[halo_base + 1, pl.ds(i, 1), :]
            for q in range(quarters):
                span = slice(q * 128, q * 128 + 128)
                grid_f[q, 8 : 8 + rows, :] = block[:, span]
                grid_f[q, 7:8, :] = first[:, span]
                grid_f[q, 8 + rows : 9 + rows, :] = last[:, span]
            for q in range(quarters):
                span = slice(q * 128, q * 128 + 128)
                for t in range(10):
                    low = grid_f[q, pl.ds(7 + t, 8, stride=8), :]
                    high = grid_f[q, pl.ds(71 + t, 8, stride=8), :]
                    tile = jnp.concatenate([low, high], 0).astype(BF16)
                    spec_ref[base + i, t * 16 : t * 16 + 16, span] = tile

    place(acq_ref, 0, 0)
    big.wait()
    place(other, dates, 2)


def pair_kernel(
    partner_ref, count_ref, low_ref, high_ref, spec_ref, even_ref, odd_ref, win_ref, out_ref, grid_f
):
    date = pl.program_id(0)
    dates = pl.num_programs(0)
    slots = out_ref.shape[1]
    mine = lax.axis_index("date") * dates + date
    live_count = count_ref[mine]
    lane = lax.broadcasted_iota(jnp.int32, (16, 128), 1)

    for j in range(slots):
        live = j < live_count
        low = jnp.where(live, low_ref[date, j], 512)
        high = high_ref[date, j]
        second = dates + lax.rem(partner_ref[mine, j], dates)
        mask_lo = ((lane >= low) & (lane < high)).astype(F32).astype(BF16)[None]
        mask_hi = ((lane + 128 >= low) & (lane + 128 < high)).astype(F32).astype(BF16)[None]
        plus, minus = [], []
        for index in (date, second):
            x = [
                spec_ref[index, :, q * 128 : q * 128 + 128].reshape(10, 16, 128)
                * (mask_lo if q % 2 == 0 else mask_hi)
                for q in range(4)
            ]
            plus.append(
                jnp.concatenate([(x[0] + x[1]).reshape(160, 128), (x[2] + x[3]).reshape(160, 128)], 1)
            )
            minus.append(
                jnp.concatenate([(x[0] - x[1]).reshape(160, 128), (x[2] - x[3]).reshape(160, 128)], 1)
            )
        fields = []
        for part, table in ((plus, even_ref), (minus, odd_ref)):
            both = jnp.dot(
                jnp.concatenate(part, 0), table[...], preferred_element_type=F32
            ).astype(BF16)
            ar, ai = both[:160, :128], both[:160, 128:]
            br, bi = both[160:, :128], both[160:, 128:]
            raw = [ar * br + ai * bi, ai * br - ar * bi, ar * ar + ai * ai, br * br + bi * bi]
            summed = []
            for f in raw:
                f = f.reshape(10, 16, 128)
                summed.append((f[0:8] + f[1:9] + f[2:10]).reshape(128, 128))
            fields.append(jnp.concatenate(summed, 0))
        looked = jnp.dot(
            jnp.concatenate(fields, 1), win_ref[...], preferred_element_type=F32
        )
        norm = lax.rsqrt(jnp.maximum(looked[256:384], 1.0) * jnp.maximum(looked[384:512], 1.0))
        for c in range(2):
            value = looked[c * 128 : c * 128 + 128] * norm
            for h in range(2):
                q = 2 * c + h
                span = slice(h * 128, h * 128 + 128)
                for t in range(8):
                    for g in range(2):
                        tile = value[t * 16 + g * 8 : t * 16 + g * 8 + 8, span]
                        grid_f[j % 2, q, pl.ds(64 * g + t, 8, stride=8), :] = tile
                out_ref[0, j, :, q * 128 : q * 128 + 128] = grid_f[j % 2, q].astype(BF16)


def local(acquisitions, partner, pair_count, band_low, band_high):
    dates, rows, cols = acquisitions.shape
    slots = partner.shape[1]
    forward, even, odd, window = tables(cols // 2)
    vmem = pl.BlockSpec(memory_space=pltpu.VMEM)
    smem = pl.BlockSpec(memory_space=pltpu.SMEM)
    spectra = pl.pallas_call(
        exchange_kernel,
        out_shape=jax.ShapeDtypeStruct((2 * dates, 160, cols), BF16),
        in_specs=[vmem, vmem],
        out_specs=vmem,
        scratch_shapes=[
            pltpu.VMEM((dates, rows, cols), BF16),
            pltpu.VMEM((2, dates, cols), F32),
            pltpu.VMEM((2, dates, cols), BF16),
            pltpu.VMEM((4, dates, cols), BF16),
            pltpu.VMEM((4, dates, cols), F32),
            pltpu.VMEM((cols // 128, rows + 16, 128), F32),
            pltpu.SemaphoreType.DMA((5,)),
            pltpu.SemaphoreType.DMA((5,)),
        ],
        compiler_params=pltpu.CompilerParams(
            collective_id=0, has_side_effects=True, vmem_limit_bytes=32 << 20
        ),
        name="exchange",
    )(acquisitions, forward)
    return pl.pallas_call(
        pair_kernel,
        grid=(dates,),
        out_shape=jax.ShapeDtypeStruct((dates, slots, rows, cols), BF16),
        in_specs=[smem, smem, smem, smem, vmem, vmem, vmem, vmem],
        out_specs=pl.BlockSpec((1, slots, rows, cols), lambda d: (d, 0, 0, 0)),
        scratch_shapes=[pltpu.VMEM((2, cols // 128, rows, 128), F32)],
        compiler_params=pltpu.CompilerParams(vmem_limit_bytes=40 << 20),
        name="pairs",
    )(partner, pair_count, band_low, band_high, spectra, even, odd, window)


def solution(mesh):
    placed = (P("date", "space", None), P(), P(), P("date", None), P("date", None))
    return jax.shard_map(
        local, mesh=mesh, in_specs=placed, out_specs=P("date", None, "space", None), check_vma=False
    )
```

```python
import functools
import math

import jax
import jax.numpy as jnp
import numpy as np
from jax import lax
from jax.experimental import pallas as pl
from jax.experimental.pallas import tpu as pltpu
from jax.sharding import PartitionSpec as P

F32 = jnp.float32
BF16 = jnp.bfloat16


def tables(bins):
    ids = np.arange(bins)
    angles = (ids[:, None] * ids[None, :] % bins) * (2.0 * math.pi / bins)
    cosine, sine = np.cos(angles), np.sin(angles)
    forward = np.block([[cosine, -sine], [sine, cosine]])
    inverse = np.block([[cosine, sine], [-sine, cosine]]) / bins
    half = bins // 2
    rows = np.concatenate([np.arange(half), bins + np.arange(half)])
    even = np.concatenate([np.arange(0, bins, 2), bins + np.arange(0, bins, 2)])
    odd = even + 1
    order = np.concatenate([np.arange(0, bins, 2), np.arange(1, bins, 2)])
    window = (np.abs(order[:, None] - ids[None, :]) <= 4).astype(np.float32)
    return (
        jnp.asarray(forward, BF16),
        jnp.asarray(inverse[rows][:, even], BF16),
        jnp.asarray(inverse[rows][:, odd], BF16),
        jnp.asarray(window, BF16),
    )


BASE = 16
PITCH = 9
MESH = pl.DeviceIdType.MESH


def segment(ref, lead, t):
    shift = {-1: -2, 8: PITCH}.get(t, t)
    parts = [ref[lead + (pl.ds(BASE + 8 * PITCH * h + shift, 8, stride=PITCH),)] for h in range(2)]
    return jnp.concatenate(parts, 0)


def band(low, high, live):
    lane = lax.broadcasted_iota(jnp.int32, (16, 128), 1)
    low = jnp.where(live, low, 512)
    return [
        ((lane + shift >= low) & (lane + shift < high)).astype(F32).astype(BF16)
        for shift in (0, 128)
    ]


def halves(tile, masks):
    x = [tile[q] * masks[q % 2] for q in range(4)]
    return (
        jnp.concatenate([x[0] + x[1], x[2] + x[3]], 1),
        jnp.concatenate([x[0] - x[1], x[2] - x[3]], 1),
    )


def front_kernel(
    acq_hbm, fwd_hbm, even_hbm, odd_hbm, low_hbm, high_hbm, count_hbm,
    far_ref, ref_ref,
    own, other, fwd, even, odd, low_s, high_s, count_s,
    edge_f, edge, halo, halo_f, nat, local_sem, send, recv,
):
    dates, rows, cols = own.shape
    slots = low_s.shape[1]
    quarters = cols // 128
    date = lax.axis_index("date")
    space = lax.axis_index("space")
    count = lax.axis_size("space")
    before = lax.rem(space + count - 1, count)
    after = lax.rem(space + 1, count)
    far = 1 - date
    has_before = space > 0
    has_after = space < count - 1

    barrier = pltpu.get_barrier_semaphore()

    def greet(peer):
        pl.semaphore_signal(barrier, inc=1, device_id=peer, device_id_type=MESH)

    greet((far, space))

    @pl.when(has_before)
    def _():
        greet((date, before))
        greet((far, before))

    @pl.when(has_after)
    def _():
        greet((date, after))
        greet((far, after))

    loads = [
        pltpu.make_async_copy(src, dst, local_sem.at[k])
        for k, (src, dst) in enumerate(
            (
                (acq_hbm, own),
                (fwd_hbm, fwd),
                (even_hbm, even),
                (odd_hbm, odd),
                (low_hbm, low_s),
                (high_hbm, high_s),
                (count_hbm, count_s),
            )
        )
    ]
    for load in loads:
        load.start()

    def remote(src, dst, k, peer):
        return pltpu.make_async_remote_copy(
            src_ref=src,
            dst_ref=dst,
            send_sem=send.at[k],
            recv_sem=recv.at[k],
            device_id=peer,
            device_id_type=MESH,
        )

    down = [remote(edge.at[1], halo.at[0], 0, (date, after)), remote(edge.at[1], halo.at[2], 2, (far, after))]
    up = [remote(edge.at[0], halo.at[1], 1, (date, before)), remote(edge.at[0], halo.at[3], 3, (far, before))]
    big = remote(own, other, 4, (far, space))

    loads[0].wait()
    for d in range(dates):
        edge_f[0, d : d + 1, :] = own[d, 0:16, :].astype(F32)[0:1]
        edge_f[1, d : d + 1, :] = own[d, rows - 16 : rows, :].astype(F32)[15:16]
    edge[...] = edge_f[...].astype(BF16)

    pl.semaphore_wait(
        barrier, 1 + 2 * has_before.astype(jnp.int32) + 2 * has_after.astype(jnp.int32)
    )
    big.start()

    @pl.when(has_after)
    def _():
        for copy in down:
            copy.start()

    @pl.when(has_before)
    def _():
        for copy in up:
            copy.start()

    def transform(source, i):
        block = jnp.dot(source[i], fwd[...], preferred_element_type=F32)
        for q in range(quarters):
            for s in range(rows // 8):
                place = slice(BASE + PITCH * s, BASE + PITCH * s + 8)
                nat[i, q, place, :] = block[8 * s : 8 * s + 8, q * 128 : q * 128 + 128]

    def references(i, tiles):
        x = [[segment(nat, (i, q), t).astype(BF16) for q in range(quarters)] for t in tiles]
        plus, minus = [], []
        first = date * dates
        for j in range(slots):
            masks = band(low_s[i, j], high_s[i, j], j < count_s[first + i])
            for tile in x:
                p, m = halves(tile, masks)
                plus.append(p)
                minus.append(m)
        for e, (part, table) in enumerate(((plus, even), (minus, odd))):
            both = jnp.dot(jnp.concatenate(part, 0), table[...], preferred_element_type=F32)
            for j in range(slots):
                for k, t in enumerate(tiles):
                    top = 16 * (j * len(tiles) + k)
                    for c in range(2):
                        ref_ref[i * slots + j, t + 1, e, c] = both[top : top + 16, 128 * c : 128 * c + 128]

    for load in loads[1:]:
        load.wait()

    @pl.loop(0, dates)
    def _(i):
        transform(own, i)

    @pl.loop(0, dates)
    def _(i):
        references(i, tuple(range(8)))

    @pl.when(has_after)
    def _():
        for copy in down:
            copy.wait_send()
        for copy in up:
            copy.wait_recv()

    @pl.when(has_before)
    def _():
        for copy in up:
            copy.wait_send()
        for copy in down:
            copy.wait_recv()

    @pl.when(jnp.logical_not(has_before))
    def _():
        halo[0] = jnp.zeros(halo.shape[1:], BF16)
        halo[2] = jnp.zeros(halo.shape[1:], BF16)

    @pl.when(jnp.logical_not(has_after))
    def _():
        halo[1] = jnp.zeros(halo.shape[1:], BF16)
        halo[3] = jnp.zeros(halo.shape[1:], BF16)

    for k in range(4):
        halo_f[k] = jnp.dot(halo[k], fwd[...], preferred_element_type=F32)

    def fringe(k):
        for i in range(dates):
            for q in range(quarters):
                span = slice(q * 128, q * 128 + 128)
                nat[i, q, BASE - 2 : BASE - 1, :] = halo_f[k, i : i + 1, span]
                nat[i, q, BASE + 16 * PITCH : BASE + 16 * PITCH + 1, :] = halo_f[k + 1, i : i + 1, span]

    fringe(0)

    @pl.loop(0, dates)
    def _(i):
        references(i, (-1, 8))

    fringe(2)
    big.wait()

    @pl.loop(0, dates)
    def _(i):
        transform(other, i)
        for q in range(quarters):
            for t in range(-1, 9):
                far_ref[i, q, 16 * t + 16 : 16 * t + 32, :] = segment(nat, (i, q), t)


def pair_kernel(
    far_ref, ref_ref, even_hbm, odd_hbm, win_hbm, partner_hbm, low_hbm, high_hbm, count_hbm,
    out_ref,
    even, odd, win, partner_s, low_s, high_s, count_s, sec0, sec1, grid0, grid1, ready, local_sem, out_sem,
):
    dates, slots = low_s.shape
    pairs = dates * slots
    depth = ready.shape[0]
    unroll = depth // 2
    first = lax.axis_index("date") * dates
    loads = [
        pltpu.make_async_copy(src, dst, local_sem.at[k])
        for k, (src, dst) in enumerate(
            (
                (even_hbm, even),
                (odd_hbm, odd),
                (win_hbm, win),
                (partner_hbm, partner_s),
                (low_hbm, low_s),
                (high_hbm, high_s),
                (count_hbm, count_s),
            )
        )
    ]
    for load in loads:
        load.start()

    def finish(p, slot):
        return pltpu.make_async_copy(
            ready.at[slot], out_ref.at[p // slots, lax.rem(p, slots)], out_sem.at[slot]
        )

    for s in range(depth):
        finish(s, s).start()
    for load in loads:
        load.wait()

    def secondary(p, buf):
        d = p // slots
        j = p - d * slots
        masks = band(low_s[d, j], high_s[d, j], j < count_s[first + d])
        index = lax.rem(partner_s[first + d, j], dates)
        plus, minus = [], []
        for t in range(10):
            tile = [far_ref[index, q, 16 * t : 16 * t + 16, :].astype(BF16) for q in range(4)]
            a, b = halves(tile, masks)
            plus.append(a)
            minus.append(b)
        for e, (part, table) in enumerate(((plus, even), (minus, odd))):
            both = jnp.dot(jnp.concatenate(part, 0), table[...], preferred_element_type=F32)
            for t in range(10):
                for c in range(2):
                    buf[t, e, c] = both[16 * t : 16 * t + 16, 128 * c : 128 * c + 128]

    def coherence(p, buf, grid, slot):
        lines, tiles = [], []
        for t in range(10):
            fields = [[], [], [], []]
            for e in range(2):
                ar, ai = (ref_ref[p, t, e, c].astype(BF16) for c in range(2))
                br, bi = (buf[t, e, c].astype(BF16) for c in range(2))
                fields[0].append(ar * br + ai * bi)
                fields[1].append(ai * br - ar * bi)
                fields[2].append(ar * ar + ai * ai)
                fields[3].append(br * br + bi * bi)
            tiles.append(fields)
            if t >= 2:
                for k in range(4):
                    three = [tiles[t - 2][k][e] + tiles[t - 1][k][e] + tiles[t][k][e] for e in range(2)]
                    lines.append(jnp.concatenate(three, 1))
        looked = jnp.dot(jnp.concatenate(lines, 0), win[...], preferred_element_type=F32)
        for t in range(8):
            cr, ci, pr, ps = (looked[64 * t + 16 * k : 64 * t + 16 * k + 16] for k in range(4))
            norm = lax.rsqrt(jnp.maximum(pr, 1.0) * jnp.maximum(ps, 1.0))
            for c, v in ((0, cr), (1, ci)):
                v = v * norm
                for h in range(2):
                    for g in range(2):
                        where = pl.ds(8 * PITCH * g + t, 8, stride=PITCH)
                        grid[2 * c + h, where, :] = v[8 * g : 8 * g + 8, 128 * h : 128 * h + 128]
        for q in range(4):
            for s in range(8):
                v = [grid[q, pl.ds(PITCH * (2 * s + g), 8), :] for g in range(2)]
                ready[slot, 16 * s : 16 * s + 16, 128 * q : 128 * q + 128] = jnp.concatenate(v, 0).astype(BF16)

    secs, grids = (sec0, sec1), (grid0, grid1)
    secondary(0, sec0)

    @pl.loop(0, pairs // unroll)
    def _(i):
        base = unroll * i
        at = [lax.rem(base + u, depth) for u in range(unroll)]
        for u in range(unroll):
            finish(base + u, at[u]).wait()
        for u in range(unroll):
            following = base + u + 1
            if u == unroll - 1:
                following = jnp.minimum(following, pairs - 1)
            secondary(following, secs[(u + 1) % 2])
            coherence(base + u, secs[u % 2], grids[u % 2], at[u])
        for u in range(unroll):
            finish(base + u, at[u]).start()

    for s in range(depth):
        finish(s, s).wait()


def local(acquisitions, partner, pair_count, band_low, band_high):
    dates, rows, cols = acquisitions.shape
    slots = partner.shape[1]
    quarters = cols // 128
    unroll = 8
    forward, even, odd, window = tables(cols // 2)
    vmem = pl.BlockSpec(memory_space=pltpu.VMEM)
    hbm = pl.BlockSpec(memory_space=pltpu.HBM)
    stay = functools.partial(pltpu.with_memory_space_constraint, memory_space=pltpu.HBM)
    forward, even, odd, window, acquisitions, partner, pair_count, band_low, band_high = (
        stay(x)
        for x in (forward, even, odd, window, acquisitions, partner, pair_count, band_low, band_high)
    )
    half = pltpu.VMEM((256, 256), BF16)
    per_slot = pltpu.SMEM((dates, slots), jnp.int32)
    far, ref = pl.pallas_call(
        front_kernel,
        out_shape=(
            jax.ShapeDtypeStruct((dates, quarters, 160, 128), F32),
            jax.ShapeDtypeStruct((dates * slots, 10, 2, 2, 16, 128), F32),
        ),
        in_specs=[hbm] * 7,
        out_specs=(vmem, vmem),
        scratch_shapes=[
            pltpu.VMEM((dates, rows, cols), BF16),
            pltpu.VMEM((dates, rows, cols), BF16),
            pltpu.VMEM((cols, cols), BF16),
            half,
            half,
            per_slot,
            per_slot,
            pltpu.SMEM(pair_count.shape, jnp.int32),
            pltpu.VMEM((2, dates, cols), F32),
            pltpu.VMEM((2, dates, cols), BF16),
            pltpu.VMEM((4, dates, cols), BF16),
            pltpu.VMEM((4, dates, cols), F32),
            pltpu.VMEM((dates, quarters, BASE + 16 * PITCH + 8, 128), F32),
            pltpu.SemaphoreType.DMA((7,)),
            pltpu.SemaphoreType.DMA((5,)),
            pltpu.SemaphoreType.DMA((5,)),
        ],
        compiler_params=pltpu.CompilerParams(
            collective_id=0, has_side_effects=True, vmem_limit_bytes=16 << 20
        ),
        name="front",
    )(acquisitions, forward, even, odd, band_low, band_high, pair_count)
    return pl.pallas_call(
        pair_kernel,
        out_shape=jax.ShapeDtypeStruct((dates, slots, rows, cols), BF16),
        in_specs=[vmem, vmem] + [hbm] * 7,
        out_specs=hbm,
        scratch_shapes=[
            half,
            half,
            half,
            pltpu.SMEM(partner.shape, jnp.int32),
            per_slot,
            per_slot,
            pltpu.SMEM(pair_count.shape, jnp.int32),
            pltpu.VMEM((10, 2, 2, 16, 128), F32),
            pltpu.VMEM((10, 2, 2, 16, 128), F32),
            pltpu.VMEM((quarters, 160, 128), F32),
            pltpu.VMEM((quarters, 160, 128), F32),
            pltpu.VMEM((2 * unroll, rows, cols), BF16),
            pltpu.SemaphoreType.DMA((7,)),
            pltpu.SemaphoreType.DMA((2 * unroll,)),
        ],
        compiler_params=pltpu.CompilerParams(vmem_limit_bytes=16 << 20),
        name="pairs",
    )(far, ref, even, odd, window, partner, band_low, band_high, pair_count)


def solution(mesh):
    placed = (P("date", "space", None), P(), P(), P("date", None), P("date", None))
    return jax.shard_map(
        local, mesh=mesh, in_specs=placed, out_specs=P("date", None, "space", None), check_vma=False
    )
```

```python
import functools
import math

import jax
import jax.numpy as jnp
import numpy as np
from jax import lax
from jax.experimental import pallas as pl
from jax.experimental.pallas import tpu as pltpu
from jax.sharding import PartitionSpec as P

F32 = jnp.float32
BF16 = jnp.bfloat16


def tables(bins):
    ids = np.arange(bins)
    angles = (ids[:, None] * ids[None, :] % bins) * (2.0 * math.pi / bins)
    cosine, sine = np.cos(angles), np.sin(angles)
    forward = np.block([[cosine, -sine], [sine, cosine]])
    inverse = np.block([[cosine, sine], [-sine, cosine]]) / bins
    half = bins // 2
    rows = np.concatenate([np.arange(half), bins + np.arange(half)])
    even = np.concatenate([np.arange(0, bins, 2), bins + np.arange(0, bins, 2)])
    odd = even + 1
    order = np.concatenate([np.arange(0, bins, 2), np.arange(1, bins, 2)])
    window = (np.abs(order[:, None] - ids[None, :]) <= 4).astype(np.float32)
    return (
        jnp.asarray(forward, BF16),
        jnp.asarray(inverse[rows][:, even], BF16),
        jnp.asarray(inverse[rows][:, odd], BF16),
        jnp.asarray(window, BF16),
    )


BASE = 16
PITCH = 9
MESH = pl.DeviceIdType.MESH


def segment(ref, lead, t):
    shift = {-1: -2, 8: PITCH}.get(t, t)
    parts = [ref[lead + (pl.ds(BASE + 8 * PITCH * h + shift, 8, stride=PITCH),)] for h in range(2)]
    return jnp.concatenate(parts, 0)


def band(low, high, live):
    lane = lax.broadcasted_iota(jnp.int32, (16, 128), 1)
    low = jnp.where(live, low, 512)
    return [
        ((lane + shift >= low) & (lane + shift < high)).astype(F32).astype(BF16)
        for shift in (0, 128)
    ]


def halves(tile, masks):
    x = [tile[q] * masks[q % 2] for q in range(4)]
    return (
        jnp.concatenate([x[0] + x[1], x[2] + x[3]], 1),
        jnp.concatenate([x[0] - x[1], x[2] - x[3]], 1),
    )


def front_kernel(
    acq_hbm, fwd_hbm, even_hbm, odd_hbm, low_hbm, high_hbm, count_hbm,
    far_ref, ref_ref,
    own, other, fwd, even, odd, low_s, high_s, count_s,
    edge_f, edge, halo, halo_f, nat, nat_far, local_sem, send, recv,
):
    dates, rows, cols = own.shape
    slots = low_s.shape[1]
    quarters = cols // 128
    date = lax.axis_index("date")
    space = lax.axis_index("space")
    count = lax.axis_size("space")
    before = lax.rem(space + count - 1, count)
    after = lax.rem(space + 1, count)
    far = 1 - date
    has_before = space > 0
    has_after = space < count - 1

    barrier = pltpu.get_barrier_semaphore()

    def greet(peer):
        pl.semaphore_signal(barrier, inc=1, device_id=peer, device_id_type=MESH)

    greet((far, space))

    @pl.when(has_before)
    def _():
        greet((date, before))
        greet((far, before))

    @pl.when(has_after)
    def _():
        greet((date, after))
        greet((far, after))

    loads = [
        pltpu.make_async_copy(src, dst, local_sem.at[k])
        for k, (src, dst) in enumerate(
            (
                (acq_hbm, own),
                (fwd_hbm, fwd),
                (even_hbm, even),
                (odd_hbm, odd),
                (low_hbm, low_s),
                (high_hbm, high_s),
                (count_hbm, count_s),
            )
        )
    ]
    for load in loads:
        load.start()

    def remote(src, dst, k, peer):
        return pltpu.make_async_remote_copy(
            src_ref=src,
            dst_ref=dst,
            send_sem=send.at[k],
            recv_sem=recv.at[k],
            device_id=peer,
            device_id_type=MESH,
        )

    down = [remote(edge.at[1], halo.at[0], 0, (date, after)), remote(edge.at[1], halo.at[2], 2, (far, after))]
    up = [remote(edge.at[0], halo.at[1], 1, (date, before)), remote(edge.at[0], halo.at[3], 3, (far, before))]
    big = remote(own, other, 4, (far, space))

    loads[0].wait()
    for d in range(dates):
        edge_f[0, d : d + 1, :] = own[d, 0:16, :].astype(F32)[0:1]
        edge_f[1, d : d + 1, :] = own[d, rows - 16 : rows, :].astype(F32)[15:16]
    edge[...] = edge_f[...].astype(BF16)

    pl.semaphore_wait(
        barrier, 1 + 2 * has_before.astype(jnp.int32) + 2 * has_after.astype(jnp.int32)
    )

    @pl.when(has_after)
    def _():
        for copy in down:
            copy.start()

    @pl.when(has_before)
    def _():
        for copy in up:
            copy.start()

    big.start()

    def transform(source, target):
        block = jnp.dot(
            source[...].reshape(dates * rows, cols), fwd[...], preferred_element_type=F32
        )
        for i in range(dates):
            for s in range(rows // 8):
                top = i * rows + 8 * s
                place = slice(BASE + PITCH * s, BASE + PITCH * s + 8)
                for q in range(quarters):
                    target[i, q, place, :] = block[top : top + 8, q * 128 : q * 128 + 128]

    def references(start, amount, tiles):
        plus, minus = [], []
        for n in range(amount):
            i = start + n
            x = [[segment(nat, (i, q), t).astype(BF16) for q in range(quarters)] for t in tiles]
            for j in range(slots):
                masks = band(low_s[i, j], high_s[i, j], j < count_s[date * dates + i])
                for tile in x:
                    p, m = halves(tile, masks)
                    plus.append(p)
                    minus.append(m)
        for e, (part, table) in enumerate(((plus, even), (minus, odd))):
            both = jnp.dot(jnp.concatenate(part, 0), table[...], preferred_element_type=F32)
            for n in range(amount * slots):
                for k, t in enumerate(tiles):
                    top = 16 * (n * len(tiles) + k)
                    for c in range(2):
                        ref_ref[start * slots + n, t + 1, e, c] = both[
                            top : top + 16, 128 * c : 128 * c + 128
                        ]

    def spread(tiles):
        @pl.loop(0, dates)
        def _(i):
            for q in range(quarters):
                for t in tiles:
                    far_ref[i, q, 16 * t + 16 : 16 * t + 32, :] = segment(nat_far, (i, q), t)

    for load in loads[1:]:
        load.wait()

    transform(own, nat)

    @pl.loop(0, dates // 2)
    def _(i):
        references(2 * i, 2, tuple(range(8)))

    big.wait()
    transform(other, nat_far)
    spread(tuple(range(8)))

    @pl.when(has_after)
    def _():
        for copy in down:
            copy.wait_send()
        for copy in up:
            copy.wait_recv()

    @pl.when(has_before)
    def _():
        for copy in up:
            copy.wait_send()
        for copy in down:
            copy.wait_recv()

    @pl.when(jnp.logical_not(has_before))
    def _():
        halo[0] = jnp.zeros(halo.shape[1:], BF16)
        halo[2] = jnp.zeros(halo.shape[1:], BF16)

    @pl.when(jnp.logical_not(has_after))
    def _():
        halo[1] = jnp.zeros(halo.shape[1:], BF16)
        halo[3] = jnp.zeros(halo.shape[1:], BF16)

    halo_f[...] = jnp.dot(
        halo[...].reshape(4 * dates, cols), fwd[...], preferred_element_type=F32
    ).reshape(4, dates, cols)
    for k, target in ((0, nat), (2, nat_far)):
        for i in range(dates):
            for q in range(quarters):
                span = slice(q * 128, q * 128 + 128)
                target[i, q, BASE - 2 : BASE - 1, :] = halo_f[k, i : i + 1, span]
                target[i, q, BASE + 16 * PITCH : BASE + 16 * PITCH + 1, :] = halo_f[k + 1, i : i + 1, span]

    @pl.loop(0, dates // 4)
    def _(i):
        references(4 * i, 4, (-1, 8))

    spread((-1, 8))


def pair_kernel(
    far_ref, ref_ref, even_hbm, odd_hbm, win_hbm, partner_hbm, low_hbm, high_hbm, count_hbm,
    out_ref,
    even, odd, win, partner_s, low_s, high_s, count_s, sec0, sec1,
    grid0, grid1, grid2, grid3, ready, local_sem, out_sem,
):
    dates, slots = low_s.shape
    pairs = dates * slots
    depth = ready.shape[0]
    unroll = depth // 2
    first = lax.axis_index("date") * dates
    loads = [
        pltpu.make_async_copy(src, dst, local_sem.at[k])
        for k, (src, dst) in enumerate(
            (
                (even_hbm, even),
                (odd_hbm, odd),
                (win_hbm, win),
                (partner_hbm, partner_s),
                (low_hbm, low_s),
                (high_hbm, high_s),
                (count_hbm, count_s),
            )
        )
    ]
    for load in loads:
        load.start()

    def finish(group, half):
        return pltpu.make_async_copy(
            ready.at[pl.ds(unroll * half, unroll)], out_ref.at[pl.ds(unroll * group, unroll)], out_sem.at[half]
        )

    finish(0, 0).start()
    for load in loads:
        load.wait()

    def secondary(p, buf):
        d = p // slots
        j = p - d * slots
        masks = band(low_s[d, j], high_s[d, j], j < count_s[first + d])
        index = lax.rem(partner_s[first + d, j], dates)
        plus, minus = [], []
        for t in range(10):
            tile = [far_ref[index, q, 16 * t : 16 * t + 16, :].astype(BF16) for q in range(4)]
            a, b = halves(tile, masks)
            plus.append(a)
            minus.append(b)
        for e, (part, table) in enumerate(((plus, even), (minus, odd))):
            both = jnp.dot(jnp.concatenate(part, 0), table[...], preferred_element_type=F32)
            for t in range(10):
                for c in range(2):
                    buf[t, e, c] = both[16 * t : 16 * t + 16, 128 * c : 128 * c + 128]

    def coherence(p, buf, grid):
        lines, tiles = [], []
        for t in range(10):
            fields = [[], [], [], []]
            for e in range(2):
                ar, ai = (ref_ref[p, t, e, c].astype(BF16) for c in range(2))
                br, bi = (buf[t, e, c].astype(BF16) for c in range(2))
                fields[0].append(ar * br + ai * bi)
                fields[1].append(ai * br - ar * bi)
                fields[2].append(ar * ar + ai * ai)
                fields[3].append(br * br + bi * bi)
            tiles.append(fields)
            if t >= 3 and t % 2:
                inner = [[tiles[t - 2][k][e] + tiles[t - 1][k][e] for e in range(2)] for k in range(4)]
                for o in (t - 3, t):
                    for k in range(4):
                        three = [inner[k][e] + tiles[o][k][e] for e in range(2)]
                        lines.append(jnp.concatenate(three, 1))
        looked = jnp.dot(jnp.concatenate(lines, 0), win[...], preferred_element_type=F32)
        for t in range(8):
            cr, ci, pr, ps = (looked[64 * t + 16 * k : 64 * t + 16 * k + 16] for k in range(4))
            norm = lax.rsqrt(jnp.maximum(pr, 1.0) * jnp.maximum(ps, 1.0))
            for c, v in ((0, cr), (1, ci)):
                v = v * norm
                for h in range(2):
                    for g in range(2):
                        where = pl.ds(8 * PITCH * g + t, 8, stride=PITCH)
                        grid[2 * c + h, where, :] = v[8 * g : 8 * g + 8, 128 * h : 128 * h + 128]

    def emit(grid, slot):
        for q in range(4):
            for s in range(8):
                v = [grid[q, pl.ds(PITCH * (2 * s + g), 8), :] for g in range(2)]
                ready[slot, 16 * s : 16 * s + 16, 128 * q : 128 * q + 128] = jnp.concatenate(v, 0).astype(BF16)

    secs, grids = (sec0, sec1), (grid0, grid1, grid2, grid3)
    groups = pairs // unroll
    last = grids[(unroll - 1) % 4]
    secondary(0, sec0)

    @pl.loop(0, groups)
    def _(i):
        base = unroll * i
        half = lax.rem(i, 2)
        finish(i, half).wait()
        emit(last, unroll * (1 - half) + unroll - 1)
        finish(lax.rem(i + groups - 1, groups), 1 - half).start()
        for u in range(unroll):
            following = base + u + 1
            if u == unroll - 1:
                following = jnp.minimum(following, pairs - 1)
            secondary(following, secs[(u + 1) % 2])
            coherence(base + u, secs[u % 2], grids[u % 4])
            if u:
                emit(grids[(u - 1) % 4], unroll * half + u - 1)

    end = (groups - 1) % 2
    emit(last, unroll * end + unroll - 1)
    finish(groups - 1, end).start()
    for half in range(2):
        finish(0, half).wait()


def local(acquisitions, partner, pair_count, band_low, band_high):
    dates, rows, cols = acquisitions.shape
    slots = partner.shape[1]
    quarters = cols // 128
    unroll = 8
    forward, even, odd, window = tables(cols // 2)
    vmem = pl.BlockSpec(memory_space=pltpu.VMEM)
    hbm = pl.BlockSpec(memory_space=pltpu.HBM)
    stay = functools.partial(pltpu.with_memory_space_constraint, memory_space=pltpu.HBM)
    forward, even, odd, window, acquisitions, partner, pair_count, band_low, band_high = (
        stay(x)
        for x in (forward, even, odd, window, acquisitions, partner, pair_count, band_low, band_high)
    )
    half = pltpu.VMEM((256, 256), BF16)
    per_slot = pltpu.SMEM((dates, slots), jnp.int32)
    far, ref = pl.pallas_call(
        front_kernel,
        out_shape=(
            jax.ShapeDtypeStruct((dates, quarters, 160, 128), F32),
            jax.ShapeDtypeStruct((dates * slots, 10, 2, 2, 16, 128), F32),
        ),
        in_specs=[hbm] * 7,
        out_specs=(vmem, vmem),
        scratch_shapes=[
            pltpu.VMEM((dates, rows, cols), BF16),
            pltpu.VMEM((dates, rows, cols), BF16),
            pltpu.VMEM((cols, cols), BF16),
            half,
            half,
            per_slot,
            per_slot,
            pltpu.SMEM(pair_count.shape, jnp.int32),
            pltpu.VMEM((2, dates, cols), F32),
            pltpu.VMEM((2, dates, cols), BF16),
            pltpu.VMEM((4, dates, cols), BF16),
            pltpu.VMEM((4, dates, cols), F32),
            pltpu.VMEM((dates, quarters, BASE + 16 * PITCH + 8, 128), F32),
            pltpu.VMEM((dates, quarters, BASE + 16 * PITCH + 8, 128), F32),
            pltpu.SemaphoreType.DMA((7,)),
            pltpu.SemaphoreType.DMA((5,)),
            pltpu.SemaphoreType.DMA((5,)),
        ],
        compiler_params=pltpu.CompilerParams(
            collective_id=0, has_side_effects=True, vmem_limit_bytes=16 << 20
        ),
        name="front",
    )(acquisitions, forward, even, odd, band_low, band_high, pair_count)
    pairs = pl.pallas_call(
        pair_kernel,
        out_shape=jax.ShapeDtypeStruct((dates * slots, rows, cols), BF16),
        in_specs=[vmem, vmem] + [hbm] * 7,
        out_specs=hbm,
        scratch_shapes=[
            half,
            half,
            half,
            pltpu.SMEM(partner.shape, jnp.int32),
            per_slot,
            per_slot,
            pltpu.SMEM(pair_count.shape, jnp.int32),
            pltpu.VMEM((10, 2, 2, 16, 128), F32),
            pltpu.VMEM((10, 2, 2, 16, 128), F32),
            *[pltpu.VMEM((quarters, 160, 128), F32)] * 4,
            pltpu.VMEM((2 * unroll, rows, cols), BF16),
            pltpu.SemaphoreType.DMA((7,)),
            pltpu.SemaphoreType.DMA((2,)),
        ],
        compiler_params=pltpu.CompilerParams(vmem_limit_bytes=16 << 20),
        name="pairs",
    )(far, ref, even, odd, window, partner, band_low, band_high, pair_count)
    return pairs.reshape(dates, slots, rows, cols)


def solution(mesh):
    placed = (P("date", "space", None), P(), P(), P("date", None), P("date", None))
    return jax.shard_map(
        local, mesh=mesh, in_specs=placed, out_specs=P("date", None, "space", None), check_vma=False
    )
```

```python
import functools
import math

import jax
import jax.numpy as jnp
import numpy as np
from jax import lax
from jax.experimental import pallas as pl
from jax.experimental.pallas import tpu as pltpu
from jax.sharding import PartitionSpec as P

F32 = jnp.float32
BF16 = jnp.bfloat16


def tables(bins):
    ids = np.arange(bins)
    angles = (ids[:, None] * ids[None, :] % bins) * (2.0 * math.pi / bins)
    cosine, sine = np.cos(angles), np.sin(angles)
    forward = np.block([[cosine, -sine], [sine, cosine]])
    inverse = np.block([[cosine, sine], [-sine, cosine]]) / bins
    half = bins // 2
    rows = np.concatenate([np.arange(half), bins + np.arange(half)])
    even = np.concatenate([np.arange(0, bins, 2), bins + np.arange(0, bins, 2)])
    odd = even + 1
    order = np.concatenate([np.arange(0, bins, 2), np.arange(1, bins, 2)])
    window = (np.abs(order[:, None] - ids[None, :]) <= 4).astype(np.float32)
    return (
        jnp.asarray(forward, BF16),
        jnp.asarray(inverse[rows][:, even], BF16),
        jnp.asarray(inverse[rows][:, odd], BF16),
        jnp.asarray(window, BF16),
    )


PITCH = 9
MESH = pl.DeviceIdType.MESH


def segment(ref, lead, t):
    parts = [ref[lead + (pl.ds(8 * PITCH * h + t, 8, stride=PITCH),)] for h in range(2)]
    return jnp.concatenate(parts, 0)


def inside(low, high):
    lane = lax.broadcasted_iota(jnp.int32, (16, 128), 1)
    return [
        ((lane + shift >= low) & (lane + shift < high)).astype(F32).astype(BF16)
        for shift in (0, 128)
    ]


def halves(tile, masks):
    x = [tile[q] * masks[q % 2] for q in range(4)]
    return (
        jnp.concatenate([x[0] + x[1], x[2] + x[3]], 1),
        jnp.concatenate([x[0] - x[1], x[2] - x[3]], 1),
    )


def front_kernel(
    acq_hbm, fwd_hbm, even_hbm, odd_hbm, win_hbm, partner_hbm, low_hbm, high_hbm, count_hbm,
    ref_ref, sec_ref, rim_ref, win_ref,
    own, other, fwd, even, odd, partner_s, low_s, high_s, count_s,
    edge_f, edge, halo, halo_f, picked, nat, nat_far, local_sem, send, recv,
):
    dates, rows, cols = own.shape
    slots = low_s.shape[1]
    quarters = cols // 128
    date = lax.axis_index("date")
    space = lax.axis_index("space")
    count = lax.axis_size("space")
    before = lax.rem(space + count - 1, count)
    after = lax.rem(space + 1, count)
    far = 1 - date
    has_before = space > 0
    has_after = space < count - 1

    barrier = pltpu.get_barrier_semaphore()

    def greet(peer):
        pl.semaphore_signal(barrier, inc=1, device_id=peer, device_id_type=MESH)

    greet((far, space))

    @pl.when(has_before)
    def _():
        greet((date, before))
        greet((far, before))

    @pl.when(has_after)
    def _():
        greet((date, after))
        greet((far, after))

    loads = [
        pltpu.make_async_copy(src, dst, local_sem.at[k])
        for k, (src, dst) in enumerate(
            (
                (acq_hbm, own),
                (fwd_hbm, fwd),
                (even_hbm, even),
                (odd_hbm, odd),
                (low_hbm, low_s),
                (high_hbm, high_s),
                (count_hbm, count_s),
                (partner_hbm, partner_s),
                (win_hbm, win_ref),
            )
        )
    ]
    for load in loads:
        load.start()

    def remote(src, dst, k, peer):
        return pltpu.make_async_remote_copy(
            src_ref=src,
            dst_ref=dst,
            send_sem=send.at[k],
            recv_sem=recv.at[k],
            device_id=peer,
            device_id_type=MESH,
        )

    down = [remote(edge.at[1], halo.at[0], 0, (date, after)), remote(edge.at[1], halo.at[2], 2, (far, after))]
    up = [remote(edge.at[0], halo.at[1], 1, (date, before)), remote(edge.at[0], halo.at[3], 3, (far, before))]
    big = remote(own, other, 4, (far, space))

    loads[0].wait()
    for d in range(dates):
        edge_f[0, d : d + 1, :] = own[d, 0:16, :].astype(F32)[0:1]
        edge_f[1, d : d + 1, :] = own[d, rows - 16 : rows, :].astype(F32)[15:16]
    edge[...] = edge_f[...].astype(BF16)

    pl.semaphore_wait(
        barrier, 1 + 2 * has_before.astype(jnp.int32) + 2 * has_after.astype(jnp.int32)
    )

    @pl.when(has_after)
    def _():
        for copy in down:
            copy.start()

    @pl.when(has_before)
    def _():
        for copy in up:
            copy.start()

    big.start()

    def transform(source, target):
        block = jnp.dot(
            source[...].reshape(dates * rows, cols), fwd[...], preferred_element_type=F32
        )
        for i in range(dates):
            for s in range(rows // 8):
                top = i * rows + 8 * s
                place = slice(PITCH * s, PITCH * s + 8)
                for q in range(quarters):
                    target[i, q, place, :] = block[top : top + 8, q * 128 : q * 128 + 128]

    first = date * dates
    steps = rows // 16

    def read(source, index):
        return [[segment(source, (index, q), t).astype(BF16) for q in range(quarters)] for t in range(steps)]

    def limits(i, j):
        return jnp.where(j < count_s[first + i], low_s[i, j], 512), high_s[i, j]

    def chosen(i, j):
        return lax.rem(partner_s[first + i, j], dates)

    def products(start, amount, out, spectra):
        plus, minus = [], []
        for n in range(amount):
            for j in range(slots):
                masks = inside(*limits(start + n, j))
                for tile in spectra(n, j):
                    p, m = halves(tile, masks)
                    plus.append(p)
                    minus.append(m)
        for e, (part, table) in enumerate(((plus, even), (minus, odd))):
            both = jnp.dot(jnp.concatenate(part, 0), table[...], preferred_element_type=F32)
            for n in range(amount * slots):
                for c in range(2):
                    out[start * slots + n, e, c] = both[rows * n : rows * n + rows, 128 * c : 128 * c + 128]

    def references(start, amount):
        x = [read(nat, start + n) for n in range(amount)]
        products(start, amount, ref_ref, lambda n, j: x[n])

    def secondaries(start, amount):
        products(start, amount, sec_ref, lambda n, j: read(nat_far, chosen(start + n, j)))

    for load in loads[1:]:
        load.wait()

    transform(own, nat)

    @pl.loop(0, dates // 2)
    def _(i):
        references(2 * i, 2)

    big.wait()
    transform(other, nat_far)

    @pl.loop(0, dates // 2)
    def _(i):
        secondaries(2 * i, 2)

    @pl.when(has_after)
    def _():
        for copy in down:
            copy.wait_send()
        for copy in up:
            copy.wait_recv()

    @pl.when(has_before)
    def _():
        for copy in up:
            copy.wait_send()
        for copy in down:
            copy.wait_recv()

    @pl.when(jnp.logical_not(has_before))
    def _():
        halo[0] = jnp.zeros(halo.shape[1:], BF16)
        halo[2] = jnp.zeros(halo.shape[1:], BF16)

    @pl.when(jnp.logical_not(has_after))
    def _():
        halo[1] = jnp.zeros(halo.shape[1:], BF16)
        halo[3] = jnp.zeros(halo.shape[1:], BF16)

    halo_f[...] = jnp.dot(
        halo[...].reshape(4 * dates, cols), fwd[...], preferred_element_type=F32
    ).reshape(4, dates, cols)
    for j in range(slots):
        for d in range(dates):
            index = chosen(d, j)
            for k in range(2):
                picked[j, dates * k + d : dates * k + d + 1, :] = halo_f[2 + k, pl.ds(index, 1), :]
    row = lax.rem(lax.broadcasted_iota(jnp.int32, (16, 128), 0), dates)
    masks = []
    for j in range(slots):
        low = high = jnp.zeros((16, 128), jnp.int32)
        for d in range(dates):
            one_low, one_high = limits(d, j)
            low = jnp.where(row == d, one_low, low)
            high = jnp.where(row == d, one_high, high)
        masks.append(inside(low, high))
    near = jnp.concatenate([halo_f[0], halo_f[1]], 0).astype(BF16)
    for k in range(2):
        plus, minus = [], []
        for j in range(slots):
            line = picked[j].astype(BF16) if k else near
            p, m = halves([line[:, 128 * q : 128 * q + 128] for q in range(quarters)], masks[j])
            plus.append(p)
            minus.append(m)
        for e, (part, table) in enumerate(((plus, even), (minus, odd))):
            both = jnp.dot(jnp.concatenate(part, 0), table[...], preferred_element_type=F32)
            for c in range(2):
                rim_ref[k, e, c] = both[:, 128 * c : 128 * c + 128]


def pair_kernel(ref_ref, sec_ref, rim_ref, win, out_ref, grid0, grid1, grid2, grid3, ready, out_sem):
    pairs = ref_ref.shape[0]
    dates = 8
    slots = pairs // dates
    sublane = lax.broadcasted_iota(jnp.int32, (8, 128), 0)
    banks, splits = out_sem.shape
    unroll = ready.shape[0] // banks
    part = unroll // splits
    groups = pairs // unroll

    def finish(group, bank):
        return [
            pltpu.make_async_copy(
                ready.at[pl.ds(unroll * bank + part * k, part)],
                out_ref.at[pl.ds(unroll * group + part * k, part)],
                out_sem.at[bank, k],
            )
            for k in range(splits)
        ]

    def start(copies):
        for copy in copies:
            copy.start()

    def wait(copies):
        for copy in copies:
            copy.wait()

    for bank in range(banks - 1):
        start(finish(bank, bank))

    def field(ref, k, p, t, e, c):
        if 0 <= t < 8:
            return ref[p, e, c, 16 * t : 16 * t + 16, :].astype(BF16)
        d = p // slots
        line = 2 * dates * (p - d * slots) + d
        if t < 0:
            low = ref[p, e, c, pl.ds(111, 8), :]
            low = jnp.where(sublane == 0, rim_ref[k, e, c, pl.ds(line, 1), :], low)
            high = ref[p, e, c, pl.ds(119, 8), :]
        else:
            low = ref[p, e, c, pl.ds(1, 8), :]
            high = ref[p, e, c, pl.ds(9, 8), :]
            high = jnp.where(sublane == 7, rim_ref[k, e, c, pl.ds(line + dates, 1), :], high)
        return jnp.concatenate([low, high], 0).astype(BF16)

    def coherence(p, grid):
        lines, tiles = [], []
        for t in range(10):
            fields = [[], [], [], []]
            for e in range(2):
                ar, ai = (field(ref_ref, 0, p, t - 1, e, c) for c in range(2))
                br, bi = (field(sec_ref, 1, p, t - 1, e, c) for c in range(2))
                fields[0].append(ar * br + ai * bi)
                fields[1].append(ai * br - ar * bi)
                fields[2].append(ar * ar + ai * ai)
                fields[3].append(br * br + bi * bi)
            tiles.append(fields)
            if t >= 3 and t % 2:
                inner = [[tiles[t - 2][k][e] + tiles[t - 1][k][e] for e in range(2)] for k in range(4)]
                for o in (t - 3, t):
                    for k in range(4):
                        three = [inner[k][e] + tiles[o][k][e] for e in range(2)]
                        lines.append(jnp.concatenate(three, 1))
        looked = jnp.dot(jnp.concatenate(lines, 0), win[...], preferred_element_type=F32)
        for t in range(8):
            cr, ci, pr, ps = (looked[64 * t + 16 * k : 64 * t + 16 * k + 16] for k in range(4))
            norm = lax.rsqrt(jnp.maximum(pr, 1.0) * jnp.maximum(ps, 1.0))
            for c, v in ((0, cr), (1, ci)):
                v = v * norm
                for h in range(2):
                    for g in range(2):
                        where = pl.ds(8 * PITCH * g + t, 8, stride=PITCH)
                        grid[2 * c + h, where, :] = v[8 * g : 8 * g + 8, 128 * h : 128 * h + 128]

    def emit(grid, slot):
        for q in range(4):
            for s in range(8):
                v = [grid[q, pl.ds(PITCH * (2 * s + g), 8), :] for g in range(2)]
                ready[slot, 16 * s : 16 * s + 16, 128 * q : 128 * q + 128] = jnp.concatenate(v, 0).astype(BF16)

    grids = (grid0, grid1, grid2, grid3)
    last = grids[(unroll - 1) % 4]

    @pl.loop(0, groups)
    def _(i):
        bank = lax.rem(i, banks)
        previous = lax.rem(i + banks - 1, banks)
        wait(finish(i, bank))
        emit(last, unroll * previous + unroll - 1)
        start(finish(lax.rem(i + groups - 1, groups), previous))
        for u in range(unroll):
            coherence(unroll * i + u, grids[u % 4])
            if u:
                emit(grids[(u - 1) % 4], unroll * bank + u - 1)

    end = (groups - 1) % banks
    emit(last, unroll * end + unroll - 1)
    start(finish(groups - 1, end))
    for bank in range(banks):
        wait(finish(0, bank))


def local(acquisitions, partner, pair_count, band_low, band_high):
    dates, rows, cols = acquisitions.shape
    slots = partner.shape[1]
    quarters = cols // 128
    unroll = 8
    forward, even, odd, window = tables(cols // 2)
    vmem = pl.BlockSpec(memory_space=pltpu.VMEM)
    hbm = pl.BlockSpec(memory_space=pltpu.HBM)
    stay = functools.partial(pltpu.with_memory_space_constraint, memory_space=pltpu.HBM)
    forward, even, odd, window, acquisitions, partner, pair_count, band_low, band_high = (
        stay(x)
        for x in (forward, even, odd, window, acquisitions, partner, pair_count, band_low, band_high)
    )
    half = pltpu.VMEM((256, 256), BF16)
    per_slot = pltpu.SMEM((dates, slots), jnp.int32)
    fields = jax.ShapeDtypeStruct((dates * slots, 2, 2, rows, 128), F32)
    rim_shape = jax.ShapeDtypeStruct((2, 2, 2, 2 * dates * slots, 128), F32)
    natural = pltpu.VMEM((dates, quarters, 16 * PITCH, 128), F32)
    ref, sec, rim, win = pl.pallas_call(
        front_kernel,
        out_shape=(fields, fields, rim_shape, jax.ShapeDtypeStruct(window.shape, BF16)),
        in_specs=[hbm] * 9,
        out_specs=(vmem, vmem, vmem, vmem),
        scratch_shapes=[
            pltpu.VMEM((dates, rows, cols), BF16),
            pltpu.VMEM((dates, rows, cols), BF16),
            pltpu.VMEM((cols, cols), BF16),
            half,
            half,
            pltpu.SMEM(partner.shape, jnp.int32),
            per_slot,
            per_slot,
            pltpu.SMEM(pair_count.shape, jnp.int32),
            pltpu.VMEM((2, dates, cols), F32),
            pltpu.VMEM((2, dates, cols), BF16),
            pltpu.VMEM((4, dates, cols), BF16),
            pltpu.VMEM((4, dates, cols), F32),
            pltpu.VMEM((slots, 2 * dates, cols), F32),
            natural,
            natural,
            pltpu.SemaphoreType.DMA((9,)),
            pltpu.SemaphoreType.DMA((5,)),
            pltpu.SemaphoreType.DMA((5,)),
        ],
        compiler_params=pltpu.CompilerParams(
            collective_id=0, has_side_effects=True, vmem_limit_bytes=14 << 20
        ),
        name="front",
    )(acquisitions, forward, even, odd, window, partner, band_low, band_high, pair_count)
    pairs = pl.pallas_call(
        pair_kernel,
        out_shape=jax.ShapeDtypeStruct((dates * slots, rows, cols), BF16),
        in_specs=[vmem, vmem, vmem, vmem],
        out_specs=hbm,
        scratch_shapes=[
            *[pltpu.VMEM((quarters, 160, 128), F32)] * 4,
            pltpu.VMEM((3 * unroll, rows, cols), BF16),
            pltpu.SemaphoreType.DMA((3, 4)),
        ],
        compiler_params=pltpu.CompilerParams(vmem_limit_bytes=14 << 20),
        name="pairs",
    )(ref, sec, rim, win)
    return pairs.reshape(dates, slots, rows, cols)


def solution(mesh):
    placed = (P("date", "space", None), P(), P(), P("date", None), P("date", None))
    return jax.shard_map(
        local, mesh=mesh, in_specs=placed, out_specs=P("date", None, "space", None), check_vma=False
    )
```

```python
import functools
import math

import jax
import jax.numpy as jnp
import numpy as np
from jax import lax
from jax.experimental import pallas as pl
from jax.experimental.pallas import tpu as pltpu
from jax.sharding import PartitionSpec as P

F32 = jnp.float32
BF16 = jnp.bfloat16


def tables(bins):
    ids = np.arange(bins)
    angles = (ids[:, None] * ids[None, :] % bins) * (2.0 * math.pi / bins)
    cosine, sine = np.cos(angles), np.sin(angles)
    forward = np.block([[cosine, -sine], [sine, cosine]])
    inverse = np.block([[cosine, sine], [-sine, cosine]]) / bins
    half = bins // 2
    rows = np.concatenate([np.arange(half), bins + np.arange(half)])
    even = np.concatenate([np.arange(0, bins, 2), bins + np.arange(0, bins, 2)])
    odd = even + 1
    order = np.concatenate([np.arange(0, bins, 2), np.arange(1, bins, 2)])
    window = (np.abs(order[:, None] - ids[None, :]) <= 4).astype(np.float32)
    return (
        jnp.asarray(forward, BF16),
        jnp.asarray(inverse[rows][:, even], BF16),
        jnp.asarray(inverse[rows][:, odd], BF16),
        jnp.asarray(window, BF16),
    )


PITCH = 9
MESH = pl.DeviceIdType.MESH


def segment(ref, lead, t):
    parts = [ref[lead + (pl.ds(8 * PITCH * h + t, 8, stride=PITCH),)] for h in range(2)]
    return jnp.concatenate(parts, 0)


def inside(low, high):
    lane = lax.broadcasted_iota(jnp.int32, (16, 128), 1)
    return [
        ((lane + shift >= low) & (lane + shift < high)).astype(F32).astype(BF16)
        for shift in (0, 128)
    ]


def halves(tile, masks):
    x = [tile[q] * masks[q % 2] for q in range(4)]
    return (
        jnp.concatenate([x[0] + x[1], x[2] + x[3]], 1),
        jnp.concatenate([x[0] - x[1], x[2] - x[3]], 1),
    )


def front_kernel(
    acq_hbm, fwd_hbm, even_hbm, odd_hbm, win_hbm, partner_hbm, low_hbm, high_hbm, count_hbm,
    ref_ref, sec_ref, rim_ref, win_ref,
    own, other, fwd, even, odd, partner_s, low_s, high_s, count_s,
    edge_f, edge, halo, halo_f, picked, nat, nat_far, local_sem, send, recv,
):
    dates, rows, cols = own.shape
    slots = low_s.shape[1]
    quarters = cols // 128
    date = lax.axis_index("date")
    space = lax.axis_index("space")
    count = lax.axis_size("space")
    before = lax.rem(space + count - 1, count)
    after = lax.rem(space + 1, count)
    far = 1 - date
    has_before = space > 0
    has_after = space < count - 1

    barrier = pltpu.get_barrier_semaphore()

    def greet(peer):
        pl.semaphore_signal(barrier, inc=1, device_id=peer, device_id_type=MESH)

    greet((far, space))

    @pl.when(has_before)
    def _():
        greet((date, before))
        greet((far, before))

    @pl.when(has_after)
    def _():
        greet((date, after))
        greet((far, after))

    loads = [
        pltpu.make_async_copy(src, dst, local_sem.at[k])
        for k, (src, dst) in enumerate(
            (
                (acq_hbm, own),
                (fwd_hbm, fwd),
                (even_hbm, even),
                (odd_hbm, odd),
                (low_hbm, low_s),
                (high_hbm, high_s),
                (count_hbm, count_s),
                (partner_hbm, partner_s),
                (win_hbm, win_ref),
            )
        )
    ]
    for load in loads:
        load.start()

    def remote(src, dst, k, peer):
        return pltpu.make_async_remote_copy(
            src_ref=src,
            dst_ref=dst,
            send_sem=send.at[k],
            recv_sem=recv.at[k],
            device_id=peer,
            device_id_type=MESH,
        )

    down = [remote(edge.at[1], halo.at[0], 0, (date, after)), remote(edge.at[1], halo.at[2], 2, (far, after))]
    up = [remote(edge.at[0], halo.at[1], 1, (date, before)), remote(edge.at[0], halo.at[3], 3, (far, before))]
    big = remote(own, other, 4, (far, space))

    loads[0].wait()
    for d in range(dates):
        edge_f[0, d : d + 1, :] = own[d, 0:16, :].astype(F32)[0:1]
        edge_f[1, d : d + 1, :] = own[d, rows - 16 : rows, :].astype(F32)[15:16]
    edge[...] = edge_f[...].astype(BF16)

    def transform(source, target):
        block = jnp.dot(
            source[...].reshape(dates * rows, cols), fwd[...], preferred_element_type=F32
        )
        for i in range(dates):
            for s in range(rows // 8):
                top = i * rows + 8 * s
                place = slice(PITCH * s, PITCH * s + 8)
                for q in range(quarters):
                    target[i, q, place, :] = block[top : top + 8, q * 128 : q * 128 + 128]

    first = date * dates
    steps = rows // 16

    def read(source, index):
        return [[segment(source, (index, q), t).astype(BF16) for q in range(quarters)] for t in range(steps)]

    def limits(i, j):
        return jnp.where(j < count_s[first + i], low_s[i, j], 512), high_s[i, j]

    def chosen(i, j):
        return lax.rem(partner_s[first + i, j], dates)

    def products(start, amount, out, spectra):
        plus, minus = [], []
        for n in range(amount):
            for j in range(slots):
                masks = inside(*limits(start + n, j))
                for tile in spectra(n, j):
                    p, m = halves(tile, masks)
                    plus.append(p)
                    minus.append(m)
        for e, (part, table) in enumerate(((plus, even), (minus, odd))):
            both = jnp.dot(jnp.concatenate(part, 0), table[...], preferred_element_type=F32)
            for n in range(amount * slots):
                for c in range(2):
                    out[start * slots + n, e, c] = both[rows * n : rows * n + rows, 128 * c : 128 * c + 128]

    def references(start, amount):
        x = [read(nat, start + n) for n in range(amount)]
        products(start, amount, ref_ref, lambda n, j: x[n])

    def secondaries(start, amount):
        products(start, amount, sec_ref, lambda n, j: read(nat_far, chosen(start + n, j)))

    for load in loads[1:]:
        load.wait()

    transform(own, nat)

    @pl.loop(0, dates // 4)
    def _(i):
        references(2 * i, 2)

    pl.semaphore_wait(
        barrier, 1 + 2 * has_before.astype(jnp.int32) + 2 * has_after.astype(jnp.int32)
    )

    @pl.when(has_after)
    def _():
        for copy in down:
            copy.start()

    @pl.when(has_before)
    def _():
        for copy in up:
            copy.start()

    big.start()

    @pl.loop(dates // 4, dates // 2)
    def _(i):
        references(2 * i, 2)

    big.wait()
    transform(other, nat_far)

    @pl.loop(0, dates // 2)
    def _(i):
        secondaries(2 * i, 2)

    @pl.when(has_after)
    def _():
        for copy in down:
            copy.wait_send()
        for copy in up:
            copy.wait_recv()

    @pl.when(has_before)
    def _():
        for copy in up:
            copy.wait_send()
        for copy in down:
            copy.wait_recv()

    @pl.when(jnp.logical_not(has_before))
    def _():
        halo[0] = jnp.zeros(halo.shape[1:], BF16)
        halo[2] = jnp.zeros(halo.shape[1:], BF16)

    @pl.when(jnp.logical_not(has_after))
    def _():
        halo[1] = jnp.zeros(halo.shape[1:], BF16)
        halo[3] = jnp.zeros(halo.shape[1:], BF16)

    halo_f[...] = jnp.dot(
        halo[...].reshape(4 * dates, cols), fwd[...], preferred_element_type=F32
    ).reshape(4, dates, cols)
    for j in range(slots):
        for d in range(dates):
            index = chosen(d, j)
            for k in range(2):
                picked[j, dates * k + d : dates * k + d + 1, :] = halo_f[2 + k, pl.ds(index, 1), :]
    row = lax.rem(lax.broadcasted_iota(jnp.int32, (16, 128), 0), dates)
    masks = []
    for j in range(slots):
        low = high = jnp.zeros((16, 128), jnp.int32)
        for d in range(dates):
            one_low, one_high = limits(d, j)
            low = jnp.where(row == d, one_low, low)
            high = jnp.where(row == d, one_high, high)
        masks.append(inside(low, high))
    near = jnp.concatenate([halo_f[0], halo_f[1]], 0).astype(BF16)
    for k in range(2):
        plus, minus = [], []
        for j in range(slots):
            line = picked[j].astype(BF16) if k else near
            p, m = halves([line[:, 128 * q : 128 * q + 128] for q in range(quarters)], masks[j])
            plus.append(p)
            minus.append(m)
        for e, (part, table) in enumerate(((plus, even), (minus, odd))):
            both = jnp.dot(jnp.concatenate(part, 0), table[...], preferred_element_type=F32)
            for c in range(2):
                rim_ref[k, e, c] = both[:, 128 * c : 128 * c + 128]


def pair_kernel(ref_ref, sec_ref, rim_ref, win, out_ref, grid0, grid1, grid2, grid3, ready, out_sem):
    pairs = ref_ref.shape[0]
    dates = 8
    slots = pairs // dates
    sublane = lax.broadcasted_iota(jnp.int32, (8, 128), 0)
    banks, splits = out_sem.shape
    unroll = ready.shape[0] // banks
    part = unroll // splits
    groups = pairs // unroll

    def finish(group, bank):
        return [
            pltpu.make_async_copy(
                ready.at[pl.ds(unroll * bank + part * k, part)],
                out_ref.at[pl.ds(unroll * group + part * k, part)],
                out_sem.at[bank, k],
            )
            for k in range(splits)
        ]

    def start(copies):
        for copy in copies:
            copy.start()

    def wait(copies):
        for copy in copies:
            copy.wait()

    for bank in range(banks - 1):
        start(finish(bank, bank))

    def field(ref, k, p, t, e, c):
        if 0 <= t < 8:
            return ref[p, e, c, 16 * t : 16 * t + 16, :].astype(BF16)
        d = p // slots
        line = 2 * dates * (p - d * slots) + d
        if t < 0:
            low = ref[p, e, c, pl.ds(111, 8), :]
            low = jnp.where(sublane == 0, rim_ref[k, e, c, pl.ds(line, 1), :], low)
            high = ref[p, e, c, pl.ds(119, 8), :]
        else:
            low = ref[p, e, c, pl.ds(1, 8), :]
            high = ref[p, e, c, pl.ds(9, 8), :]
            high = jnp.where(sublane == 7, rim_ref[k, e, c, pl.ds(line + dates, 1), :], high)
        return jnp.concatenate([low, high], 0).astype(BF16)

    def coherence(p, grid):
        lines, tiles = [], []
        for t in range(10):
            fields = [[], [], [], []]
            for e in range(2):
                ar, ai = (field(ref_ref, 0, p, t - 1, e, c) for c in range(2))
                br, bi = (field(sec_ref, 1, p, t - 1, e, c) for c in range(2))
                fields[0].append(ar * br + ai * bi)
                fields[1].append(ai * br - ar * bi)
                fields[2].append(ar * ar + ai * ai)
                fields[3].append(br * br + bi * bi)
            tiles.append(fields)
            if t >= 3 and t % 2:
                inner = [[tiles[t - 2][k][e] + tiles[t - 1][k][e] for e in range(2)] for k in range(4)]
                for o in (t - 3, t):
                    for k in range(4):
                        three = [inner[k][e] + tiles[o][k][e] for e in range(2)]
                        lines.append(jnp.concatenate(three, 1))
        looked = jnp.dot(jnp.concatenate(lines, 0), win[...], preferred_element_type=F32)
        for t in range(8):
            cr, ci, pr, ps = (looked[64 * t + 16 * k : 64 * t + 16 * k + 16] for k in range(4))
            norm = lax.rsqrt(jnp.maximum(pr, 1.0) * jnp.maximum(ps, 1.0))
            for c, v in ((0, cr), (1, ci)):
                v = v * norm
                for h in range(2):
                    for g in range(2):
                        where = pl.ds(8 * PITCH * g + t, 8, stride=PITCH)
                        grid[2 * c + h, where, :] = v[8 * g : 8 * g + 8, 128 * h : 128 * h + 128]

    def emit(grid, slot):
        for q in range(4):
            for s in range(8):
                v = [grid[q, pl.ds(PITCH * (2 * s + g), 8), :] for g in range(2)]
                ready[slot, 16 * s : 16 * s + 16, 128 * q : 128 * q + 128] = jnp.concatenate(v, 0).astype(BF16)

    grids = (grid0, grid1, grid2, grid3)
    last = grids[(unroll - 1) % 4]

    @pl.loop(0, groups)
    def _(i):
        bank = lax.rem(i, banks)
        previous = lax.rem(i + banks - 1, banks)
        wait(finish(i, bank))
        emit(last, unroll * previous + unroll - 1)
        start(finish(lax.rem(i + groups - 1, groups), previous))
        for u in range(unroll):
            coherence(unroll * i + u, grids[u % 4])
            if u:
                emit(grids[(u - 1) % 4], unroll * bank + u - 1)

    end = (groups - 1) % banks
    emit(last, unroll * end + unroll - 1)
    start(finish(groups - 1, end))
    for bank in range(banks):
        wait(finish(0, bank))


def local(acquisitions, partner, pair_count, band_low, band_high):
    dates, rows, cols = acquisitions.shape
    slots = partner.shape[1]
    quarters = cols // 128
    unroll = 8
    forward, even, odd, window = tables(cols // 2)
    vmem = pl.BlockSpec(memory_space=pltpu.VMEM)
    hbm = pl.BlockSpec(memory_space=pltpu.HBM)
    stay = functools.partial(pltpu.with_memory_space_constraint, memory_space=pltpu.HBM)
    forward, even, odd, window, acquisitions, partner, pair_count, band_low, band_high = (
        stay(x)
        for x in (forward, even, odd, window, acquisitions, partner, pair_count, band_low, band_high)
    )
    half = pltpu.VMEM((256, 256), BF16)
    per_slot = pltpu.SMEM((dates, slots), jnp.int32)
    fields = jax.ShapeDtypeStruct((dates * slots, 2, 2, rows, 128), F32)
    rim_shape = jax.ShapeDtypeStruct((2, 2, 2, 2 * dates * slots, 128), F32)
    natural = pltpu.VMEM((dates, quarters, 16 * PITCH, 128), F32)
    ref, sec, rim, win = pl.pallas_call(
        front_kernel,
        out_shape=(fields, fields, rim_shape, jax.ShapeDtypeStruct(window.shape, BF16)),
        in_specs=[hbm] * 9,
        out_specs=(vmem, vmem, vmem, vmem),
        scratch_shapes=[
            pltpu.VMEM((dates, rows, cols), BF16),
            pltpu.VMEM((dates, rows, cols), BF16),
            pltpu.VMEM((cols, cols), BF16),
            half,
            half,
            pltpu.SMEM(partner.shape, jnp.int32),
            per_slot,
            per_slot,
            pltpu.SMEM(pair_count.shape, jnp.int32),
            pltpu.VMEM((2, dates, cols), F32),
            pltpu.VMEM((2, dates, cols), BF16),
            pltpu.VMEM((4, dates, cols), BF16),
            pltpu.VMEM((4, dates, cols), F32),
            pltpu.VMEM((slots, 2 * dates, cols), F32),
            natural,
            natural,
            pltpu.SemaphoreType.DMA((9,)),
            pltpu.SemaphoreType.DMA((5,)),
            pltpu.SemaphoreType.DMA((5,)),
        ],
        compiler_params=pltpu.CompilerParams(
            collective_id=0, has_side_effects=True, vmem_limit_bytes=14 << 20
        ),
        name="front",
    )(acquisitions, forward, even, odd, window, partner, band_low, band_high, pair_count)
    pairs = pl.pallas_call(
        pair_kernel,
        out_shape=jax.ShapeDtypeStruct((dates * slots, rows, cols), BF16),
        in_specs=[vmem, vmem, vmem, vmem],
        out_specs=hbm,
        scratch_shapes=[
            *[pltpu.VMEM((quarters, 160, 128), F32)] * 4,
            pltpu.VMEM((3 * unroll, rows, cols), BF16),
            pltpu.SemaphoreType.DMA((3, 4)),
        ],
        compiler_params=pltpu.CompilerParams(vmem_limit_bytes=14 << 20),
        name="pairs",
    )(ref, sec, rim, win)
    return pairs.reshape(dates, slots, rows, cols)


def solution(mesh):
    placed = (P("date", "space", None), P(), P(), P("date", None), P("date", None))
    return jax.shard_map(
        local, mesh=mesh, in_specs=placed, out_specs=P("date", None, "space", None), check_vma=False
    )
```

```python
import functools
import math

import jax
import jax.numpy as jnp
import numpy as np
from jax import lax
from jax.experimental import pallas as pl
from jax.experimental.pallas import tpu as pltpu
from jax.sharding import PartitionSpec as P

F32 = jnp.float32
BF16 = jnp.bfloat16


def tables(bins):
    ids = np.arange(bins)
    angles = (ids[:, None] * ids[None, :] % bins) * (2.0 * math.pi / bins)
    cosine, sine = np.cos(angles), np.sin(angles)
    forward = np.block([[cosine, -sine], [sine, cosine]])
    inverse = np.block([[cosine, sine], [-sine, cosine]]) / bins
    half = bins // 2
    rows = np.concatenate([np.arange(half), bins + np.arange(half)])
    even = np.concatenate([np.arange(0, bins, 2), bins + np.arange(0, bins, 2)])
    odd = even + 1
    order = np.concatenate([np.arange(0, bins, 2), np.arange(1, bins, 2)])
    window = (np.abs(order[:, None] - ids[None, :]) <= 4).astype(np.float32)
    return (
        jnp.asarray(forward, BF16),
        jnp.asarray(inverse[rows][:, even], BF16),
        jnp.asarray(inverse[rows][:, odd], BF16),
        jnp.asarray(window, BF16),
    )


PITCH = 9
MESH = pl.DeviceIdType.MESH


def segment(ref, lead, t):
    parts = [ref[lead + (pl.ds(8 * PITCH * h + t, 8, stride=PITCH),)] for h in range(2)]
    return jnp.concatenate(parts, 0)


def inside(low, high):
    lane = lax.broadcasted_iota(jnp.int32, (16, 128), 1)
    return [
        ((lane + shift >= low) & (lane + shift < high)).astype(F32).astype(BF16)
        for shift in (0, 128)
    ]


def halves(tile, masks):
    x = [tile[q] * masks[q % 2] for q in range(4)]
    return (
        jnp.concatenate([x[0] + x[1], x[2] + x[3]], 1),
        jnp.concatenate([x[0] - x[1], x[2] - x[3]], 1),
    )


def front_kernel(
    acq_hbm, fwd_hbm, even_hbm, odd_hbm, win_hbm, partner_hbm, low_hbm, high_hbm, count_hbm,
    ref_ref, sec_ref, rim_ref, win_ref,
    own, other, fwd, even, odd, partner_s, low_s, high_s, count_s,
    edge_f, edge, halo, halo_f, picked, nat, nat_far, local_sem, send, recv,
):
    dates, rows, cols = own.shape
    slots = low_s.shape[1]
    quarters = cols // 128
    date = lax.axis_index("date")
    space = lax.axis_index("space")
    count = lax.axis_size("space")
    before = lax.rem(space + count - 1, count)
    after = lax.rem(space + 1, count)
    far = 1 - date
    has_before = space > 0
    has_after = space < count - 1

    barrier = pltpu.get_barrier_semaphore()

    def greet(peer):
        pl.semaphore_signal(barrier, inc=1, device_id=peer, device_id_type=MESH)

    greet((far, space))

    @pl.when(has_before)
    def _():
        greet((date, before))
        greet((far, before))

    @pl.when(has_after)
    def _():
        greet((date, after))
        greet((far, after))

    loads = [
        pltpu.make_async_copy(src, dst, local_sem.at[k])
        for k, (src, dst) in enumerate(
            (
                (acq_hbm, own),
                (fwd_hbm, fwd),
                (even_hbm, even),
                (odd_hbm, odd),
                (low_hbm, low_s),
                (high_hbm, high_s),
                (count_hbm, count_s),
                (partner_hbm, partner_s),
                (win_hbm, win_ref),
            )
        )
    ]
    for load in loads:
        load.start()

    def remote(src, dst, k, peer):
        return pltpu.make_async_remote_copy(
            src_ref=src,
            dst_ref=dst,
            send_sem=send.at[k],
            recv_sem=recv.at[k],
            device_id=peer,
            device_id_type=MESH,
        )

    down = [remote(edge.at[1], halo.at[0], 0, (date, after)), remote(edge.at[1], halo.at[2], 2, (far, after))]
    up = [remote(edge.at[0], halo.at[1], 1, (date, before)), remote(edge.at[0], halo.at[3], 3, (far, before))]
    chunk = dates // 2
    big = [
        remote(own.at[pl.ds(chunk * k, chunk)], other.at[pl.ds(chunk * k, chunk)], 4 + k, (far, space))
        for k in range(2)
    ]

    loads[0].wait()
    for d in range(dates):
        edge_f[0, d : d + 1, :] = own[d, 0:16, :].astype(F32)[0:1]
        edge_f[1, d : d + 1, :] = own[d, rows - 16 : rows, :].astype(F32)[15:16]
    edge[...] = edge_f[...].astype(BF16)

    def transform(source, target, start, amount):
        block = jnp.dot(
            source[start : start + amount].reshape(amount * rows, cols), fwd[...], preferred_element_type=F32
        )
        for i in range(start, start + amount):
            for s in range(rows // 8):
                top = (i - start) * rows + 8 * s
                place = slice(PITCH * s, PITCH * s + 8)
                for q in range(quarters):
                    target[i, q, place, :] = block[top : top + 8, q * 128 : q * 128 + 128]

    first = date * dates
    steps = rows // 16

    def read(source, index):
        return [[segment(source, (index, q), t).astype(BF16) for q in range(quarters)] for t in range(steps)]

    def limits(i, j):
        return jnp.where(j < count_s[first + i], low_s[i, j], 512), high_s[i, j]

    def chosen(i, j):
        return lax.rem(partner_s[first + i, j], dates)

    def products(start, amount, out, spectra):
        plus, minus = [], []
        for n in range(amount):
            for j in range(slots):
                masks = inside(*limits(start + n, j))
                for tile in spectra(n, j):
                    p, m = halves(tile, masks)
                    plus.append(p)
                    minus.append(m)
        for e, (part, table) in enumerate(((plus, even), (minus, odd))):
            both = jnp.dot(jnp.concatenate(part, 0), table[...], preferred_element_type=F32)
            for n in range(amount * slots):
                for c in range(2):
                    out[start * slots + n, e, c] = both[rows * n : rows * n + rows, 128 * c : 128 * c + 128]

    def references(start, amount):
        x = [read(nat, start + n) for n in range(amount)]
        products(start, amount, ref_ref, lambda n, j: x[n])

    def secondaries(start, amount):
        products(start, amount, sec_ref, lambda n, j: read(nat_far, chosen(start + n, j)))

    for load in loads[1:]:
        load.wait()

    transform(own, nat, 0, dates)

    @pl.loop(0, dates // 4)
    def _(i):
        references(2 * i, 2)

    pl.semaphore_wait(
        barrier, 1 + 2 * has_before.astype(jnp.int32) + 2 * has_after.astype(jnp.int32)
    )

    @pl.when(has_after)
    def _():
        for copy in down:
            copy.start()

    @pl.when(has_before)
    def _():
        for copy in up:
            copy.start()

    for copy in big:
        copy.start()

    @pl.loop(dates // 4, dates // 2)
    def _(i):
        references(2 * i, 2)

    for k in range(2):
        big[k].wait()
        transform(other, nat_far, chunk * k, chunk)

    @pl.loop(0, dates // 2)
    def _(i):
        secondaries(2 * i, 2)

    @pl.when(has_after)
    def _():
        for copy in down:
            copy.wait_send()
        for copy in up:
            copy.wait_recv()

    @pl.when(has_before)
    def _():
        for copy in up:
            copy.wait_send()
        for copy in down:
            copy.wait_recv()

    @pl.when(jnp.logical_not(has_before))
    def _():
        halo[0] = jnp.zeros(halo.shape[1:], BF16)
        halo[2] = jnp.zeros(halo.shape[1:], BF16)

    @pl.when(jnp.logical_not(has_after))
    def _():
        halo[1] = jnp.zeros(halo.shape[1:], BF16)
        halo[3] = jnp.zeros(halo.shape[1:], BF16)

    halo_f[...] = jnp.dot(
        halo[...].reshape(4 * dates, cols), fwd[...], preferred_element_type=F32
    ).reshape(4, dates, cols)
    for j in range(slots):
        for d in range(dates):
            index = chosen(d, j)
            for k in range(2):
                picked[j, dates * k + d : dates * k + d + 1, :] = halo_f[2 + k, pl.ds(index, 1), :]
    row = lax.rem(lax.broadcasted_iota(jnp.int32, (16, 128), 0), dates)
    masks = []
    for j in range(slots):
        low = high = jnp.zeros((16, 128), jnp.int32)
        for d in range(dates):
            one_low, one_high = limits(d, j)
            low = jnp.where(row == d, one_low, low)
            high = jnp.where(row == d, one_high, high)
        masks.append(inside(low, high))
    near = jnp.concatenate([halo_f[0], halo_f[1]], 0).astype(BF16)
    for k in range(2):
        plus, minus = [], []
        for j in range(slots):
            line = picked[j].astype(BF16) if k else near
            p, m = halves([line[:, 128 * q : 128 * q + 128] for q in range(quarters)], masks[j])
            plus.append(p)
            minus.append(m)
        for e, (part, table) in enumerate(((plus, even), (minus, odd))):
            both = jnp.dot(jnp.concatenate(part, 0), table[...], preferred_element_type=F32)
            for c in range(2):
                rim_ref[k, e, c] = both[:, 128 * c : 128 * c + 128]


def pair_kernel(ref_ref, sec_ref, rim_ref, win, out_ref, grid0, grid1, grid2, grid3, ready, out_sem):
    pairs = ref_ref.shape[0]
    dates = 8
    slots = pairs // dates
    sublane = lax.broadcasted_iota(jnp.int32, (8, 128), 0)
    banks, splits = out_sem.shape
    unroll = ready.shape[0] // banks
    part = unroll // splits
    groups = pairs // unroll

    def finish(group, bank):
        return [
            pltpu.make_async_copy(
                ready.at[pl.ds(unroll * bank + part * k, part)],
                out_ref.at[pl.ds(unroll * group + part * k, part)],
                out_sem.at[bank, k],
            )
            for k in range(splits)
        ]

    def start(copies):
        for copy in copies:
            copy.start()

    def wait(copies):
        for copy in copies:
            copy.wait()

    for bank in range(banks):
        start(finish(bank, bank)[: splits - 1 if bank == banks - 1 else splits])

    def field(ref, k, p, t, e, c):
        if 0 <= t < 8:
            return ref[p, e, c, 16 * t : 16 * t + 16, :].astype(BF16)
        d = p // slots
        line = 2 * dates * (p - d * slots) + d
        if t < 0:
            low = ref[p, e, c, pl.ds(111, 8), :]
            low = jnp.where(sublane == 0, rim_ref[k, e, c, pl.ds(line, 1), :], low)
            high = ref[p, e, c, pl.ds(119, 8), :]
        else:
            low = ref[p, e, c, pl.ds(1, 8), :]
            high = ref[p, e, c, pl.ds(9, 8), :]
            high = jnp.where(sublane == 7, rim_ref[k, e, c, pl.ds(line + dates, 1), :], high)
        return jnp.concatenate([low, high], 0).astype(BF16)

    def coherence(p, grid):
        lines, tiles = [], []
        for t in range(10):
            fields = [[], [], [], []]
            for e in range(2):
                ar, ai = (field(ref_ref, 0, p, t - 1, e, c) for c in range(2))
                br, bi = (field(sec_ref, 1, p, t - 1, e, c) for c in range(2))
                fields[0].append(ar * br + ai * bi)
                fields[1].append(ai * br - ar * bi)
                fields[2].append(ar * ar + ai * ai)
                fields[3].append(br * br + bi * bi)
            tiles.append(fields)
            if t >= 3 and t % 2:
                inner = [[tiles[t - 2][k][e] + tiles[t - 1][k][e] for e in range(2)] for k in range(4)]
                for o in (t - 3, t):
                    for k in range(4):
                        three = [inner[k][e] + tiles[o][k][e] for e in range(2)]
                        lines.append(jnp.concatenate(three, 1))
        looked = jnp.dot(jnp.concatenate(lines, 0), win[...], preferred_element_type=F32)
        for t in range(8):
            cr, ci, pr, ps = (looked[64 * t + 16 * k : 64 * t + 16 * k + 16] for k in range(4))
            norm = lax.rsqrt(jnp.maximum(pr, 1.0) * jnp.maximum(ps, 1.0))
            for c, v in ((0, cr), (1, ci)):
                v = v * norm
                for h in range(2):
                    for g in range(2):
                        where = pl.ds(8 * PITCH * g + t, 8, stride=PITCH)
                        grid[2 * c + h, where, :] = v[8 * g : 8 * g + 8, 128 * h : 128 * h + 128]

    def emit(grid, slot):
        for q in range(4):
            for s in range(8):
                v = [grid[q, pl.ds(PITCH * (2 * s + g), 8), :] for g in range(2)]
                ready[slot, 16 * s : 16 * s + 16, 128 * q : 128 * q + 128] = jnp.concatenate(v, 0).astype(BF16)

    grids = (grid0, grid1, grid2, grid3)
    last = grids[(unroll - 1) % 4]

    @pl.loop(0, groups)
    def _(i):
        bank = lax.rem(i, banks)
        previous = lax.rem(i + banks - 1, banks)
        wait(finish(i, bank))
        emit(last, unroll * previous + unroll - 1)
        start(finish(lax.rem(i + groups - 1, groups), previous)[splits - 1 :])
        for u in range(unroll):
            coherence(unroll * i + u, grids[u % 4])
            if u:
                emit(grids[(u - 1) % 4], unroll * bank + u - 1)
                if u % part == 0:
                    start(finish(i, bank)[u // part - 1 : u // part])

    end = (groups - 1) % banks
    emit(last, unroll * end + unroll - 1)
    start(finish(groups - 1, end)[splits - 1 :])
    for bank in range(banks):
        wait(finish(0, bank))


def local(acquisitions, partner, pair_count, band_low, band_high):
    dates, rows, cols = acquisitions.shape
    slots = partner.shape[1]
    quarters = cols // 128
    unroll = 8
    forward, even, odd, window = tables(cols // 2)
    vmem = pl.BlockSpec(memory_space=pltpu.VMEM)
    hbm = pl.BlockSpec(memory_space=pltpu.HBM)
    stay = functools.partial(pltpu.with_memory_space_constraint, memory_space=pltpu.HBM)
    forward, even, odd, window, acquisitions, partner, pair_count, band_low, band_high = (
        stay(x)
        for x in (forward, even, odd, window, acquisitions, partner, pair_count, band_low, band_high)
    )
    half = pltpu.VMEM((256, 256), BF16)
    per_slot = pltpu.SMEM((dates, slots), jnp.int32)
    fields = jax.ShapeDtypeStruct((dates * slots, 2, 2, rows, 128), F32)
    rim_shape = jax.ShapeDtypeStruct((2, 2, 2, 2 * dates * slots, 128), F32)
    natural = pltpu.VMEM((dates, quarters, 16 * PITCH, 128), F32)
    ref, sec, rim, win = pl.pallas_call(
        front_kernel,
        out_shape=(fields, fields, rim_shape, jax.ShapeDtypeStruct(window.shape, BF16)),
        in_specs=[hbm] * 9,
        out_specs=(vmem, vmem, vmem, vmem),
        scratch_shapes=[
            pltpu.VMEM((dates, rows, cols), BF16),
            pltpu.VMEM((dates, rows, cols), BF16),
            pltpu.VMEM((cols, cols), BF16),
            half,
            half,
            pltpu.SMEM(partner.shape, jnp.int32),
            per_slot,
            per_slot,
            pltpu.SMEM(pair_count.shape, jnp.int32),
            pltpu.VMEM((2, dates, cols), F32),
            pltpu.VMEM((2, dates, cols), BF16),
            pltpu.VMEM((4, dates, cols), BF16),
            pltpu.VMEM((4, dates, cols), F32),
            pltpu.VMEM((slots, 2 * dates, cols), F32),
            natural,
            natural,
            pltpu.SemaphoreType.DMA((9,)),
            pltpu.SemaphoreType.DMA((6,)),
            pltpu.SemaphoreType.DMA((6,)),
        ],
        compiler_params=pltpu.CompilerParams(
            collective_id=0, has_side_effects=True, vmem_limit_bytes=14 << 20
        ),
        name="front",
    )(acquisitions, forward, even, odd, window, partner, band_low, band_high, pair_count)
    pairs = pl.pallas_call(
        pair_kernel,
        out_shape=jax.ShapeDtypeStruct((dates * slots, rows, cols), BF16),
        in_specs=[vmem, vmem, vmem, vmem],
        out_specs=hbm,
        scratch_shapes=[
            *[pltpu.VMEM((quarters, 160, 128), F32)] * 4,
            pltpu.VMEM((3 * unroll, rows, cols), BF16),
            pltpu.SemaphoreType.DMA((3, 4)),
        ],
        compiler_params=pltpu.CompilerParams(vmem_limit_bytes=14 << 20),
        name="pairs",
    )(ref, sec, rim, win)
    return pairs.reshape(dates, slots, rows, cols)


def solution(mesh):
    placed = (P("date", "space", None), P(), P(), P("date", None), P("date", None))
    return jax.shard_map(
        local, mesh=mesh, in_specs=placed, out_specs=P("date", None, "space", None), check_vma=False
    )
```
